32 devices in a mesh: seq: 16 (over z, x, core), head: 2 (over y).
Axes of the slice: x: 2, y: 2, z: 4, core: 2. Of those that a mesh axis runs over, the one named last changes fastest.
Arguments:
- fw_query: bfloat16 [6144, 4096], P('seq', 'head'), may hold values from -6 to 6
- fw_key: bfloat16 [6144, 4096], P('seq', 'head'), may hold values from -6 to 6
- fw_value: bfloat16 [6144, 4096], P('seq', 'head'), may hold values from -6 to 6
- learn_rate: float32 [6144, 8], P('seq', 'head'), may hold values from 0.00025515517 to 0.002551552
- fast_weights: bfloat16 [3, 8, 512, 512], P(None, 'head'), may hold values from -0.25 to 0.25
- attn_query: bfloat16 [6144, 4096], P(('seq', 'head')), may hold values from -32 to 32
- attn_key: bfloat16 [6144, 1024], P(('seq', 'head')), may hold values from -32 to 32
- attn_value: bfloat16 [6144, 1024], P(('seq', 'head')), may hold values from -6 to 6
Outputs:
- mixed: bfloat16 [6144, 4096], P(('seq', 'head'))
The draws below stay inside these ranges and needn't reach their ends.
All inputs are finite; a program needn't handle non-finite values.
Results may differ from the reference program's by a relative error of at most 0.01.
Values may be sent and summed in bfloat16 or wider, within the bound.
A program may use at most 128 MiB of HBM per device.

```python
import math
import jax
import jax.numpy as jnp
from jax import lax

FW_HEADS = 8
FW_DIM = 512
Q_HEADS = 32
KV_HEADS = 8
HEAD_DIM = 128
WINDOW = 256
D = 4096
TOKENS = 6144


def draw_attn_key(key, part):
    base = jax.random.normal(jax.random.fold_in(key, 1), (TOKENS, KV_HEADS * HEAD_DIM), jnp.float32)
    base = jnp.clip(base, -6.0, 6.0)
    return jnp.clip(base, -32.0, 32.0).astype(jnp.bfloat16)


def draw_attn_query(key, part):
    base = jax.random.normal(jax.random.fold_in(key, 2), (TOKENS, Q_HEADS * HEAD_DIM), jnp.float32)
    base = jnp.clip(base, -6.0, 6.0)
    return jnp.clip(base, -32.0, 32.0).astype(jnp.bfloat16)


def shard_levels(stream_key, dims, shards, least, top_value):
    loudness = 1.0
    for dim, blocks in shards:
        draws = jax.random.uniform(jax.random.fold_in(jax.random.fold_in(stream_key, 6), dim), (blocks,), jnp.float32, least / len(shards), top_value / len(shards))
        loudness = loudness * jnp.repeat(jnp.exp(draws), dims[dim] // blocks).reshape((-1,) + (1,) * (len(dims) - 1 - dim))
    return loudness


def noise(rng, shape, scale, most, cuts=(), kind=jnp.bfloat16):
    level = shard_levels(rng, shape, cuts, -0.22, 0.18) if cuts else 1.0
    drawn = jax.random.normal(rng, shape, jnp.float32) * scale * level
    return jnp.minimum(jnp.maximum(drawn, -most), most).astype(kind)


def setup_inputs(seed: int = 0) -> dict:
    key_of = jax.random.split(jax.random.key(seed), 9)
    return {
        "fw_query": noise(key_of[0], (TOKENS, D), 1.0, 6.0, ((0, 16), (1, 2))),
        "fw_key": noise(key_of[1], (TOKENS, D), 1.0, 6.0, ((0, 16), (1, 2))),
        "fw_value": noise(key_of[2], (TOKENS, D), 1.0, 6.0, ((0, 16), (1, 2))),
        "learn_rate": jnp.clip(jnp.exp(math.log(0.002551552) - 2.3025852 * jax.random.uniform(key_of[3], (TOKENS, FW_HEADS), jnp.float32) ** shard_levels(key_of[3], (TOKENS, FW_HEADS), ((0, 16), (1, 2)), -0.2, 0.2)), 0.00025515517, 0.002551552),
        "fast_weights": noise(key_of[4], (3, FW_HEADS, FW_DIM, FW_DIM), FW_DIM ** -0.5, 0.25, ((1, 2),)),
        "attn_query": draw_attn_query(jax.random.fold_in(key_of[8], 71), 0),
        "attn_key": draw_attn_key(jax.random.fold_in(key_of[8], 71), 0),
        "attn_value": noise(key_of[7], (TOKENS, KV_HEADS * HEAD_DIM), 1.0, 6.0, ((0, 32),)),
    }


def head_update(q, k, v, rates, weights):
    w_gate = weights[0]
    w_up = weights[1]
    w_down = weights[2]
    pre_gate = jnp.dot(k, w_gate, preferred_element_type=jnp.float32)
    pre_up = jnp.dot(k, w_up, preferred_element_type=jnp.float32)
    sigm = jax.nn.sigmoid(pre_gate)
    hidden = (pre_gate * sigm * pre_up).astype(jnp.bfloat16)
    scaled = (rates[:, None] * v.astype(jnp.float32)).astype(jnp.bfloat16)
    back = jnp.dot(scaled, w_down.T, preferred_element_type=jnp.float32)
    d_gate = (back * pre_up * sigm * (1.0 + pre_gate * (1.0 - sigm))).astype(jnp.bfloat16)
    d_up = (back * pre_gate * sigm).astype(jnp.bfloat16)
    grads = jnp.stack([jnp.dot(k.T, d_gate, preferred_element_type=jnp.float32), jnp.dot(k.T, d_up, preferred_element_type=jnp.float32), jnp.dot(hidden.T, scaled, preferred_element_type=jnp.float32)])
    start = weights.astype(jnp.float32)
    stepped = start + grads
    ratio = jnp.sqrt(lax.optimization_barrier(jnp.mean(start * start, axis=-2, keepdims=True))) * lax.rsqrt(lax.optimization_barrier(jnp.mean(stepped * stepped, axis=-2, keepdims=True)) + 1e-06)
    fresh = (stepped * ratio).astype(jnp.bfloat16)
    q_gate = jnp.dot(q, fresh[0], preferred_element_type=jnp.float32)
    q_up = jnp.dot(q, fresh[1], preferred_element_type=jnp.float32)
    answer_hidden = (q_gate * jax.nn.sigmoid(q_gate) * q_up).astype(jnp.bfloat16)
    return jnp.dot(answer_hidden, fresh[2], preferred_element_type=jnp.float32).astype(jnp.bfloat16)

def reference(fw_query, fw_key, fw_value, learn_rate, fast_weights, attn_query, attn_key, attn_value):

    def heads_first(arr):
        return arr.reshape(TOKENS, FW_HEADS, FW_DIM).transpose(1, 0, 2)

    def per_head(items):
        return head_update(items[0], items[1], items[2], items[3], items[4])
    fw_heads = lax.map(per_head, (heads_first(fw_query), heads_first(fw_key), heads_first(fw_value), learn_rate.T, fast_weights.transpose(1, 0, 2, 3)))
    fw_out = fw_heads.transpose(1, 0, 2).reshape(TOKENS, D)
    group = Q_HEADS // KV_HEADS
    block_rows = math.gcd(512, TOKENS)
    scaling = 1.0 / math.sqrt(HEAD_DIM)
    query_heads = attn_query.reshape(TOKENS, KV_HEADS, group, HEAD_DIM)
    front = jnp.zeros((WINDOW, KV_HEADS * HEAD_DIM), jnp.bfloat16)
    key_pad = jnp.concatenate([front, attn_key], axis=0).reshape(TOKENS + WINDOW, KV_HEADS, HEAD_DIM)
    value_pad = jnp.concatenate([front, attn_value], axis=0).reshape(TOKENS + WINDOW, KV_HEADS, HEAD_DIM)

    def block(index):
        start = (index * block_rows).astype(jnp.int32)
        q_block = lax.dynamic_slice_in_dim(query_heads, start, block_rows, 0)
        k_block = lax.dynamic_slice_in_dim(key_pad, start, block_rows + WINDOW, 0)
        v_block = lax.dynamic_slice_in_dim(value_pad, start, block_rows + WINDOW, 0)
        scores = jnp.einsum('fcgd,lcd->cgfl', q_block.astype(jnp.float32), k_block.astype(jnp.float32)) * scaling
        t_pos = start + jnp.arange(block_rows, dtype=jnp.int32)
        s_pos = start - WINDOW + jnp.arange(block_rows + WINDOW, dtype=jnp.int32)
        gap = t_pos[:, None] - s_pos[None, :]
        keep = (gap >= 0) & (gap < WINDOW) & (s_pos[None, :] >= 0)
        scores = jnp.where(keep, scores, -1e+30)
        top = lax.optimization_barrier(jnp.max(scores, axis=-1, keepdims=True))
        expo = jnp.exp(scores - top)
        probs = (expo / lax.optimization_barrier(jnp.sum(expo, axis=-1, keepdims=True))).astype(jnp.bfloat16)
        out = jnp.einsum('cgfl,lcd->fcgd', probs.astype(jnp.float32), v_block.astype(jnp.float32))
        return out.reshape(block_rows, Q_HEADS * HEAD_DIM)
    attn_out = lax.map(block, jnp.arange(TOKENS // block_rows, dtype=jnp.int32)).reshape(TOKENS, D)
    return (attn_out + fw_out.astype(jnp.float32)).astype(jnp.bfloat16)
```

```python
import functools
import math

import jax
import jax.numpy as jnp
from jax import lax
from jax.experimental import pallas as pl
from jax.experimental.pallas import tpu as pltpu
from jax.sharding import PartitionSpec as P

Q_HEADS = 32
KV_HEADS = 8
HEAD_DIM = 128
WINDOW = 256


def shifted(value, axis, by):
    devices = lax.axis_size(axis)
    pairs = [(i, i + by) for i in range(devices) if 0 <= i + by < devices]
    return lax.ppermute(value, axis, pairs)


def local_grads(keys, values, rates, weights):
    pre_gate = jnp.einsum("thd,hde->the", keys, weights[0], preferred_element_type=jnp.float32)
    pre_up = jnp.einsum("thd,hde->the", keys, weights[1], preferred_element_type=jnp.float32)
    sigm = jax.nn.sigmoid(pre_gate)
    hidden = (pre_gate * sigm * pre_up).astype(jnp.bfloat16)
    scaled = (rates[:, :, None] * values.astype(jnp.float32)).astype(jnp.bfloat16)
    back = jnp.einsum("the,hde->thd", scaled, weights[2], preferred_element_type=jnp.float32)
    d_gate = (back * pre_up * sigm * (1.0 + pre_gate * (1.0 - sigm))).astype(jnp.bfloat16)
    d_up = (back * pre_gate * sigm).astype(jnp.bfloat16)
    grad_gate = jnp.einsum("thd,the->hde", keys, d_gate, preferred_element_type=jnp.float32)
    grad_up = jnp.einsum("thd,the->hde", keys, d_up, preferred_element_type=jnp.float32)
    grad_down = jnp.einsum("thd,the->hde", hidden, scaled, preferred_element_type=jnp.float32)
    return jnp.stack([grad_gate, grad_up, grad_down])


def renorm(summed, start_weights):
    start = start_weights.astype(jnp.float32)
    stepped = start + summed
    ratio = jnp.sqrt(jnp.mean(start * start, axis=-2, keepdims=True)) * lax.rsqrt(
        jnp.mean(stepped * stepped, axis=-2, keepdims=True) + 1e-06
    )
    return (stepped * ratio).astype(jnp.bfloat16)


def on_device(
    fw_query, fw_key, fw_value, learn_rate, fast_weights, attn_query, attn_key, attn_value
):
    tok_rows = fw_key.shape[0]
    local_heads = fast_weights.shape[1]
    width = fast_weights.shape[2]
    keys = fw_key.reshape(tok_rows, local_heads, width)
    values = fw_value.reshape(tok_rows, local_heads, width)
    queries = fw_query.reshape(tok_rows, local_heads, width)
    grads = local_grads(keys, values, learn_rate, fast_weights)
    share = lax.psum_scatter(grads, "seq", scatter_dimension=3, tiled=True)
    columns = share.shape[3]
    start_cols = lax.dynamic_slice_in_dim(fast_weights, lax.axis_index("seq") * columns, columns, 3)
    fresh_part = renorm(share, start_cols)
    fresh = lax.all_gather(fresh_part, "seq", axis=3, tiled=True)
    q_gate = jnp.einsum("thd,hde->the", queries, fresh[0], preferred_element_type=jnp.float32)
    q_up = jnp.einsum("thd,hde->the", queries, fresh[1], preferred_element_type=jnp.float32)
    answer_hidden = (q_gate * jax.nn.sigmoid(q_gate) * q_up).astype(jnp.bfloat16)
    fw_out = jnp.einsum(
        "the,hef->thf", answer_hidden, fresh[2], preferred_element_type=jnp.float32
    ).astype(jnp.bfloat16)
    fw_out = fw_out.reshape(tok_rows, local_heads * width)
    fw_fine = lax.all_to_all(fw_out, "head", split_axis=0, concat_axis=1, tiled=True)
    rows = attn_query.shape[0]
    reach = -(-WINDOW // rows)
    kv_width = attn_key.shape[1]
    group = Q_HEADS // KV_HEADS
    buffer_k = jnp.zeros(((reach + 1) * rows, kv_width), jnp.bfloat16)
    buffer_v = jnp.zeros(((reach + 1) * rows, kv_width), jnp.bfloat16)
    buffer_k = lax.dynamic_update_slice_in_dim(buffer_k, attn_key, reach * rows, 0)
    buffer_v = lax.dynamic_update_slice_in_dim(buffer_v, attn_value, reach * rows, 0)

    def bring(step, carry):
        piece_k, piece_v, store_k, store_v = carry
        piece_k, piece_v = shifted((piece_k, piece_v), ("seq", "head"), 1)
        slot = (reach - 1 - step) * rows
        store_k = lax.dynamic_update_slice_in_dim(store_k, piece_k, slot, 0)
        store_v = lax.dynamic_update_slice_in_dim(store_v, piece_v, slot, 0)
        return (piece_k, piece_v, store_k, store_v)

    carried = lax.fori_loop(0, reach, bring, (attn_key, attn_value, buffer_k, buffer_v))
    buffer_k = carried[2].reshape((reach + 1) * rows, KV_HEADS, HEAD_DIM)
    buffer_v = carried[3].reshape((reach + 1) * rows, KV_HEADS, HEAD_DIM)
    device_pos = lax.axis_index("seq") * lax.axis_size("head") + lax.axis_index("head")
    t_pos = device_pos * rows + jnp.arange(rows, dtype=jnp.int32)
    s_pos = (device_pos - reach) * rows + jnp.arange((reach + 1) * rows, dtype=jnp.int32)
    gap = t_pos[:, None] - s_pos[None, :]
    keep = (gap >= 0) & (gap < WINDOW) & (s_pos[None, :] >= 0)
    query_heads = attn_query.reshape(rows, KV_HEADS, group, HEAD_DIM)
    scaling = 1.0 / math.sqrt(HEAD_DIM)
    scores = (
        jnp.einsum("fcgd,lcd->cgfl", query_heads, buffer_k, preferred_element_type=jnp.float32)
        * scaling
    )
    scores = jnp.where(keep, scores, -1e30)
    top = jnp.max(scores, axis=-1, keepdims=True)
    expo = jnp.exp(scores - top)
    probs = (expo / jnp.sum(expo, axis=-1, keepdims=True)).astype(jnp.bfloat16)
    attn_out = jnp.einsum("cgfl,lcd->fcgd", probs, buffer_v, preferred_element_type=jnp.float32)
    attn_out = attn_out.reshape(rows, Q_HEADS * HEAD_DIM)
    return (attn_out + fw_fine.astype(jnp.float32)).astype(jnp.bfloat16)

MESH = pl.DeviceIdType.MESH
LANES = 128
SPLIT = 1
LAG_A = 2
ROOT_B = 5
ROOT_A = 5
FIRST_ATT = 4
PREPARE = 2
DIRECT = 4
RELAY_AT = 1


def piece(p):
    return p // 3, p % 3


def fused_kernel(
    heads, width, rows,
    q_hbm, k_hbm, v_hbm, rate_hbm, w_hbm, aq_hbm, ak_hbm, av_hbm, out_ref,
    qb, kb, vb, wb, aqb, akb, avb, g, r0, rxa, rza, rxb, rzb, nw, att, bias, hidb, fsend, frecv, rate_ref, rates, via,
    in_sem, misc_sem, halo_s, halo_r, s0_s, s0_r, xa_s, xa_r, za_s, za_r, xb_s, xb_r, zb_s, zb_r,
    gax_s, gax_r, gaz_s, gaz_r, gbx_s, gbx_r, gbz_s, gbz_r, c_s, c_r, y_s, y_r, via_s, via_r, on_s,
):
    me = lax.axis_index("seq")
    y = lax.axis_index("head")
    n_seq, n_head = lax.axis_size("seq"), lax.axis_size("head")
    core, xx, z = me % 2, (me // 2) % 2, me // 4
    top = n_seq // 4 - 1
    place = z + core * (top - 2 * z)
    cb = core * 2 + xx
    ob = core * 2 + 1 - xx
    other_core = me + 1 - 2 * core
    other_x = me + 2 - 4 * xx
    ahead = me + 4 - 8 * core
    behind = me - 4 + 8 * core
    pos = me * n_head + y
    last = n_seq * n_head
    extra = WINDOW - rows
    pad = akb.shape[0] - WINDOW - rows
    half = 2 * LANES
    pairs = heads // 2
    pieces = pairs * 3
    is_root = place == top

    def cols(block, size=LANES):
        return pl.ds(pl.multiple_of(block * size, size), size)

    def remote(src, dst, ssem, rsem, seq, head=None):
        return pltpu.make_async_remote_copy(
            src_ref=src, dst_ref=dst, send_sem=ssem, recv_sem=rsem,
            device_id={"seq": seq, "head": y if head is None else head},
            device_id_type=MESH,
        )

    def loads(h):
        c = cols(h, width)
        return (
            pltpu.make_async_copy(k_hbm.at[:, c], kb.at[:, c], in_sem.at[h, 0]),
            pltpu.make_async_copy(v_hbm.at[:, c], vb.at[:, c], in_sem.at[h, 1]),
            pltpu.make_async_copy(w_hbm.at[:, h], wb.at[:, h], in_sem.at[h, 2]),
        )

    own_at = pl.ds(pad + WINDOW, rows)
    others = (
        pltpu.make_async_copy(aq_hbm, aqb, misc_sem.at[0]),
        pltpu.make_async_copy(ak_hbm, akb.at[own_at], misc_sem.at[1]),
        pltpu.make_async_copy(av_hbm, avb.at[own_at], misc_sem.at[2]),
        pltpu.make_async_copy(q_hbm, qb, misc_sem.at[3]),
    )
    rate_load = pltpu.make_async_copy(rate_hbm, rate_ref, misc_sem.at[4])
    rate_load.start()
    for i in range(heads):
        for copy in loads(i + 1 - 2 * (i % 2)):
            copy.start()
    for copy in others:
        copy.start()

    barrier = pltpu.get_barrier_semaphore()

    def greet(seq, head):
        pl.semaphore_signal(barrier, inc=1, device_id={"seq": seq, "head": head}, device_id_type=MESH)

    for seq in (other_core, other_x):
        greet(seq, y)
    greet(me, 1 - y)
    below = jnp.where(z > 0, 1, 0)
    above = jnp.where(z < top, 1, 0)

    @pl.when(z > 0)
    def _():
        greet(me - 4, y)

    @pl.when(z < top)
    def _():
        greet(me + 4, y)

    met = 3 + below + above
    for step in (1, 2):
        met = met + jnp.where(pos >= step, 1, 0) + jnp.where(pos + step < last, 1, 0)

        @pl.when(pos + step < last)
        def _():
            greet((pos + step) // n_head, (pos + step) % n_head)

        @pl.when(pos >= step)
        def _():
            greet((pos - step) // n_head, (pos - step) % n_head)

    def halo(step, c):
        there = pos + step
        seq, head = there // n_head, there % n_head
        if step == 1:
            src, dst = pl.ds(0, rows), pl.ds(pad + extra, rows)
        else:
            src, dst = pl.ds(rows - extra, extra), pl.ds(pad, extra)
        j = (step - 1) * 2
        return (
            remote(ak_hbm.at[src, cols(c)], akb.at[dst, cols(c)], halo_s.at[j, c], halo_r.at[j, c], seq, head),
            remote(av_hbm.at[src, cols(c)], avb.at[dst, cols(c)], halo_s.at[j + 1, c], halo_r.at[j + 1, c], seq, head),
        )

    across = core * y
    late = KV_HEADS - DIRECT
    late_cols = pl.ds(DIRECT * LANES, late * LANES)

    def spare(k):
        hbm = (ak_hbm, av_hbm)[k]
        return remote(hbm.at[:, late_cols], via.at[k], via_s.at[k], via_r.at[k], me, 1 - y)

    def onward(k, i):
        ref = (akb, avb)[k]
        at = cols(DIRECT + i)
        return remote(
            via.at[k, :, cols(i)], ref.at[pl.ds(pad + extra, rows), at],
            on_s.at[k, i], halo_r.at[k, DIRECT + i], (pos + 2) // n_head, (pos + 2) % n_head,
        )

    is_source = (across == 1) & (pos + 1 < last)
    is_relay = (core == 1) & (y == 0) & (pos + 2 < last)

    def halo_here(step, c):
        if step == 2:
            return pos + 2 < last
        return (pos + 1 < last) & ((c < DIRECT) | (across == 0))

    def halo_start(c, _):
        @pl.when(halo_here(1, c))
        def _():
            for copy in halo(1, c):
                copy.start()

        return 0

    def halo_start_far(c, _):
        @pl.when(halo_here(2, c))
        def _():
            for copy in halo(2, c):
                copy.start()

        return 0

    def relay_start():
        @pl.when(is_source)
        def _():
            for k in range(2):
                spare(k).start()

    def relay_on():
        @pl.when(is_relay)
        def _():
            for k in range(2):
                spare(k).wait_recv()
            for i in range(late):
                for k in range(2):
                    onward(k, i).start()

    depth = width // SPLIT
    bands = range(SPLIT)

    def band(q):
        return pl.ds(q * depth, depth)

    def f32(value):
        return value.astype(jnp.float32)

    def s0(h, m):
        return remote(g.at[h, m, :, cols(1 - core, half)], r0.at[h, m], s0_s.at[h, m], s0_r.at[h, m], other_core)

    def xa(p, q):
        hs, m = piece(p)
        return remote(
            g.at[2 * hs, m, band(q), cols(ob)], rxa.at[p, band(q)], xa_s.at[p, q], xa_r.at[p, q], other_x
        )

    def za(p, q):
        hs, m = piece(p)
        return remote(
            g.at[2 * hs, m, band(q), cols(cb)], rza.at[p, band(q)], za_s.at[p, q], za_r.at[p, q], ahead
        )

    def xb(p, q):
        hs, m = piece(p)
        return remote(
            g.at[2 * hs + 1, m, band(q), cols(ob)], rxb.at[p, band(q)], xb_s.at[p, q], xb_r.at[p, q], other_x
        )

    def zb(p, j, q):
        hs, m = piece(p)
        return remote(
            g.at[2 * hs + 1, m, band(q), cols(core * 2 + j)], rzb.at[p, j, band(q)],
            zb_s.at[p, j, q], zb_r.at[p, j, q], ahead,
        )

    def fresh(h, m, block, q):
        return nw.at[h, m, band(q), cols(block)]

    def gax(p, block, q):
        hs, m = piece(p)
        ref = fresh(2 * hs, m, block, q)
        return remote(ref, ref, gax_s.at[p, q], gax_r.at[p, q], other_x)

    def gaz(p, q):
        hs, m = piece(p)
        ref = fresh(2 * hs, m, cb, q)
        return remote(ref, ref, gaz_s.at[p, q], gaz_r.at[p, q], behind)

    def gbx(p, block, q):
        hs, m = piece(p)
        ref = fresh(2 * hs + 1, m, block, q)
        return remote(ref, ref, gbx_s.at[p, q], gbx_r.at[p, q], other_x)

    def gbz(p, j, q):
        hs, m = piece(p)
        ref = fresh(2 * hs + 1, m, core * 2 + j, q)
        return remote(ref, ref, gbz_s.at[p, j, q], gbz_r.at[p, j, q], behind)

    def pair(h, m, j, q):
        ref = fresh(h, m, core * 2 + j, q)
        return remote(ref, ref, c_s.at[h, m, j, q], c_r.at[h, m, j, q], other_core)

    def pair_from(h, m, j, q):
        ref = fresh(h, m, (1 - core) * 2 + j, q)
        return remote(ref, ref, c_s.at[h, m, j, q], c_r.at[h, m, j, q], other_core)

    def compute(h, send=True):
        for copy in loads(h):
            copy.wait()
        c = cols(h, width)
        keys = kb[:, c]
        rate = rates[h][:, :1]
        scaled = (rate * f32(vb[:, c])).astype(jnp.bfloat16)
        pre_gate = jnp.dot(keys, wb[0, h], preferred_element_type=jnp.float32)
        pre_up = jnp.dot(keys, wb[1, h], preferred_element_type=jnp.float32)
        back = lax.dot_general(
            scaled, wb[2, h], (((1,), (1,)), ((), ())), preferred_element_type=jnp.float32
        )
        sigm = jax.nn.sigmoid(pre_gate)
        tn = (((0,), (0,)), ((), ()))

        def put(m, left, right):
            g[h, m] = lax.dot_general(left, right, tn, preferred_element_type=jnp.float32).astype(g.dtype)
            if send:
                s0(h, m).start()

        d_gate = (back * pre_up * sigm * (1.0 + pre_gate * (1.0 - sigm))).astype(jnp.bfloat16)
        put(0, keys, d_gate)
        d_up = (back * pre_gate * sigm).astype(jnp.bfloat16)
        put(1, keys, d_up)
        hidden = (pre_gate * sigm * pre_up).astype(jnp.bfloat16)
        put(2, hidden, scaled)

    def own(h, m, block, part, q):
        return f32(g[h, m, band(q), cols(block)]) + f32(r0[h, m, band(q), cols(part)])

    def keep_sum(h, m, block, q, value):
        g[h, m, band(q), cols(block)] = value.astype(g.dtype)

    def finish(h, m, total):
        start = f32(wb[m, h, :, cols(cb)])
        stepped = start + total
        ratio = jnp.sqrt(jnp.mean(start * start, axis=0, keepdims=True)) * lax.rsqrt(
            jnp.mean(stepped * stepped, axis=0, keepdims=True) + 1e-06
        )
        nw[h, m, :, cols(cb)] = (stepped * ratio).astype(nw.dtype)

    def own_whole(h, m):
        return f32(g[h, m, :, cols(cb)]) + f32(r0[h, m, :, cols(xx)])

    def stage_in(p):
        hs, m = piece(p)
        h = 2 * hs
        s0(h + 1, m).wait_recv()

        @pl.when(place == 0)
        def _():
            for j in range(2):
                for q in bands:
                    keep_sum(h + 1, m, core * 2 + j, q, own(h + 1, m, core * 2 + j, j, q))
                    zb(p, j, q).start()

        s0(h, m).wait_recv()
        for q in bands:
            keep_sum(h, m, ob, q, own(h, m, ob, 1 - xx, q))
            xa(p, q).start()

    def stage_b(p):
        hs, m = piece(p)
        h = 2 * hs + 1

        @pl.when(place < top)
        def _():
            for j in range(2):
                for q in bands:
                    zb(p, j, q).wait_recv()
                    keep_sum(h, m, core * 2 + j, q, own(h, m, core * 2 + j, j, q) + f32(rzb[p, j, band(q)]))
                    zb(p, j, q).start()

        @pl.when(is_root)
        def _():
            for q in bands:
                zb(p, 1 - xx, q).wait_recv()
                keep_sum(h, m, ob, q, own(h, m, ob, 1 - xx, q) + f32(rzb[p, 1 - xx, band(q)]))
                xb(p, q).start()
            for q in bands:
                zb(p, xx, q).wait_recv()

    def stage_a(p):
        hs, m = piece(p)
        h = 2 * hs

        @pl.when(place == 0)
        def _():
            for q in bands:
                xa(p, q).wait_recv()
                keep_sum(h, m, cb, q, own(h, m, cb, xx, q) + f32(rxa[p, band(q)]))
                za(p, q).start()

        @pl.when((place > 0) & (place < top))
        def _():
            for q in bands:
                xa(p, q).wait_recv()
                za(p, q).wait_recv()
                keep_sum(h, m, cb, q, own(h, m, cb, xx, q) + f32(rxa[p, band(q)]) + f32(rza[p, band(q)]))
                za(p, q).start()

        @pl.when(is_root)
        def _():
            for q in bands:
                xa(p, q).wait_recv()
                za(p, q).wait_recv()

    def stage_root_a(p):
        hs, m = piece(p)
        h = 2 * hs
        finish(h, m, own_whole(h, m) + f32(rxa[p]) + f32(rza[p]))
        for q in bands:
            gaz(p, q).start()
            gax(p, cb, q).start()
            pair(h, m, xx, q).start()

    def stage_root_b(p):
        hs, m = piece(p)
        h = 2 * hs + 1
        for q in bands:
            xb(p, q).wait_recv()
        finish(h, m, own_whole(h, m) + f32(rzb[p, xx]) + f32(rxb[p]))
        for q in bands:
            gbx(p, cb, q).start()
            gbz(p, xx, q).start()
            pair(h, m, xx, q).start()

    def stage_down_a(p):
        hs, m = piece(p)
        for q in bands:
            gaz(p, q).wait_recv()

            @pl.when(place > 0)
            def _():
                gaz(p, q).start()

            gax(p, cb, q).start()
            pair(2 * hs, m, xx, q).start()

    def stage_down_b(p):
        hs, m = piece(p)
        for q in bands:
            gbz(p, xx, q).wait_recv()

            @pl.when(place > 0)
            def _():
                gbz(p, xx, q).start()

            pair(2 * hs + 1, m, xx, q).start()

    def stage_last_b(p):
        hs, m = piece(p)
        for q in bands:
            @pl.when(is_root)
            def _():
                gbx(p, ob, q).wait_recv()
                gbz(p, 1 - xx, q).start()

            @pl.when(place < top)
            def _():
                gbz(p, 1 - xx, q).wait_recv()

                @pl.when(place > 0)
                def _():
                    gbz(p, 1 - xx, q).start()

            pair(2 * hs + 1, m, 1 - xx, q).start()

    def stage_last_a(p):
        hs, m = piece(p)
        for q in bands:
            gax(p, ob, q).wait_recv()
            pair(2 * hs, m, 1 - xx, q).start()

    group = Q_HEADS // KV_HEADS
    scaling = 1.0 / math.sqrt(HEAD_DIM)

    def attend(c):
        for step in (1, 2):
            @pl.when(pos >= step)
            def _():
                for copy in halo(step, c):
                    copy.wait_recv()

        keys = akb[:, cols(c)]
        vals = avb[:, cols(c)]
        for j in range(group):
            qc = cols(c * group + j)
            scores = lax.dot_general(
                aqb[:, qc], keys, (((1,), (1,)), ((), ())), preferred_element_type=jnp.float32
            ) * scaling
            scores = jnp.where(bias[...] > 0.0, scores, -1e30)
            peak = jnp.max(scores, axis=-1, keepdims=True)
            expo = jnp.exp(scores - peak)
            probs = (expo / jnp.sum(expo, axis=-1, keepdims=True)).astype(jnp.bfloat16)
            att[:, qc] = jnp.dot(probs, vals, preferred_element_type=jnp.float32)

    def answer_send(h, block):
        return remote(
            fsend.at[h, :, cols(block)], frecv.at[h, :, cols(block)], y_s.at[h, block], y_r.at[h, block], me, 1 - y
        )

    def mix(value, group_of, h, block):
        at = cols((group_of * heads + h) * 4 + block)
        out_ref[:, at] = (att[:, at] + f32(value)).astype(out_ref.dtype)

    def landed(h, m, j):
        for q in bands:
            pair_from(h, m, j, q).wait_recv()

    def answer_hidden(h):
        for m in range(2):
            for j in range(2):
                landed(h, m, j)
        queries = qb[:, cols(h, width)]
        q_gate = jnp.dot(queries, nw[h, 0], preferred_element_type=jnp.float32)
        q_up = jnp.dot(queries, nw[h, 1], preferred_element_type=jnp.float32)
        hidb[h] = (q_gate * jax.nn.sigmoid(q_gate) * q_up).astype(jnp.bfloat16)

    near_half = place // 2
    early = core * near_half + (1 - core) * (1 - near_half)

    def answer(h, i):
        side = early + (i // 2) * (1 - 2 * early)
        j = xx + (i % 2) * (1 - 2 * xx)
        block = side * 2 + j

        @pl.when(side != core)
        def _():
            landed(h, 2, j)

        part = jnp.dot(hidb[h], nw[h, 2, :, cols(block)], preferred_element_type=jnp.float32).astype(jnp.bfloat16)
        low, high = f32(part[:rows]), f32(part[rows:])
        lower = jnp.zeros((rows, LANES), jnp.int32) + y < 1
        fsend[h, :, cols(block)] = jnp.where(lower, high, low).astype(jnp.bfloat16)
        answer_send(h, block).start()
        mix(jnp.where(lower, low, high), y, h, block)

    def during(p, stage):
        @pl.when((p >= 0) & (p < pieces))
        def _():
            stage(p)

    rate_load.wait()
    for h in range(heads):
        rates[h] = jnp.broadcast_to(rate_ref[h : h + 1, :], (LANES, rate_ref.shape[1])).T
    compute(1, send=False)
    pl.semaphore_wait(barrier, met)
    for m in range(3):
        s0(1, m).start()
    relay_start()
    lax.fori_loop(0, KV_HEADS, halo_start, 0)
    lax.fori_loop(0, KV_HEADS, halo_start_far, 0)
    compute(0)

    def prepare():
        for step in (1, 2):
            @pl.when(pos < step)
            def _():
                at = pl.ds(pad + extra, rows) if step == 1 else pl.ds(pad, extra)
                akb[at, :] = jnp.zeros((at.size, akb.shape[1]), akb.dtype)
                avb[at, :] = jnp.zeros((at.size, avb.shape[1]), avb.dtype)

        akb[pl.ds(0, pad), :] = jnp.zeros((pad, akb.shape[1]), akb.dtype)
        avb[pl.ds(0, pad), :] = jnp.zeros((pad, avb.shape[1]), avb.dtype)
        t_idx = lax.broadcasted_iota(jnp.int32, bias.shape, 0)
        s_idx = lax.broadcasted_iota(jnp.int32, bias.shape, 1) - (pad + WINDOW)
        gap = t_idx - s_idx
        keep = (gap >= 0) & (gap < WINDOW) & (s_idx + pos * rows >= 0)
        bias[...] = keep.astype(jnp.float32)
        for copy in others:
            copy.wait()

    done = 2 + max(ROOT_A, ROOT_B) + top + 2
    ticks = pieces + max(ROOT_A, ROOT_B) + (n_seq // 4 - 1) + 1

    def tick(t, _):
        during(t, stage_in)

        @pl.when(t < heads - 2)
        def _():
            compute(heads - 1 - t)

        @pl.when(t == RELAY_AT)
        def _():
            relay_on()

        @pl.when(place > 0)
        def _():
            during(t - place, stage_b)

        during(t - LAG_A - place, stage_a)

        @pl.when(is_root)
        def _():
            during(t - ROOT_B, stage_root_b)
            during(t - ROOT_A, stage_root_a)

        @pl.when(place < top)
        def _():
            during(t - ROOT_A - top + place, stage_down_a)
            during(t - ROOT_B - top + place, stage_down_b)

        during(t - ROOT_B - 1 - top + place, stage_last_b)
        during(t - ROOT_A - 1 - top + place, stage_last_a)

        @pl.when(t == PREPARE)
        def _():
            prepare()

        @pl.when((t >= FIRST_ATT) & (t < FIRST_ATT + KV_HEADS))
        def _():
            attend(t - FIRST_ATT)

        @pl.when((t >= done) & (t < done + 2))
        def _():
            h = t - done
            answer_hidden(h)

            def one(i, _):
                answer(h, i)
                return 0

            lax.fori_loop(0, 4, one, 0)

        return 0

    lax.fori_loop(0, ticks, tick, 0)

    def tail_hidden(h, _):
        answer_hidden(h)
        return 0

    lax.fori_loop(2, heads, tail_hidden, 0)

    def tail_answer(i, _):
        answer(2 + i % 2, i // 2)
        return 0

    lax.fori_loop(0, 8, tail_answer, 0)

    def arrive(i, _):
        h, k = i // 4, i % 4
        side = early + (k // 2) * (1 - 2 * early)
        block = side * 2 + xx + (k % 2) * (1 - 2 * xx)
        answer_send(h, block).wait_recv()
        mix(frecv[h, :, cols(block)], 1 - y, h, block)
        return 0

    lax.fori_loop(0, heads * 4, arrive, 0)

    def sent_halo(c, _):
        for step in (1, 2):
            @pl.when(halo_here(step, c))
            def _():
                for copy in halo(step, c):
                    copy.wait_send()
        return 0

    lax.fori_loop(0, KV_HEADS, sent_halo, 0)

    @pl.when(is_source)
    def _():
        for k in range(2):
            spare(k).wait_send()

    @pl.when(is_relay)
    def _():
        for k in range(2):
            for i in range(late):
                onward(k, i).wait_send()

    def sent(p, _):
        hs, m = piece(p)
        for k in range(2):
            s0(2 * hs + k, m).wait_send()
        for q in bands:
            xa(p, q).wait_send()
            gax(p, cb, q).wait_send()
            for k in range(2):
                for j in range(2):
                    pair(2 * hs + k, m, j, q).wait_send()

        @pl.when(place < top)
        def _():
            for q in bands:
                za(p, q).wait_send()
                for j in range(2):
                    zb(p, j, q).wait_send()

        @pl.when(place > 0)
        def _():
            for q in bands:
                gaz(p, q).wait_send()
                for j in range(2):
                    gbz(p, j, q).wait_send()

        @pl.when(is_root)
        def _():
            for q in bands:
                xb(p, q).wait_send()
                gbx(p, cb, q).wait_send()

        return 0

    lax.fori_loop(0, pieces, sent, 0)

    def sent_y(i, _):
        answer_send(i // 4, i % 4).wait_send()
        return 0

    lax.fori_loop(0, heads * 4, sent_y, 0)


def fused(fw_query, fw_key, fw_value, learn_rate, fast_weights, attn_query, attn_key, attn_value):
    tokens, heads, width = fw_key.shape[0], fast_weights.shape[1], fast_weights.shape[2]
    rows, kv_width = attn_key.shape
    span = -(-(WINDOW + rows) // LANES) * LANES
    bf, f32 = jnp.bfloat16, jnp.float32
    anywhere = pl.BlockSpec(memory_space=pl.ANY)
    vmem = pl.BlockSpec(memory_space=pltpu.VMEM)
    dma = pltpu.SemaphoreType.DMA
    pieces = heads // 2 * 3
    return pl.pallas_call(
        functools.partial(fused_kernel, heads, width, rows),
        out_shape=pltpu.VMEM(attn_query.shape, bf),
        in_specs=[anywhere, anywhere, anywhere, anywhere, anywhere, anywhere, anywhere, anywhere],
        out_specs=vmem,
        scratch_shapes=[
            pltpu.VMEM(fw_query.shape, bf),
            pltpu.VMEM(fw_key.shape, bf),
            pltpu.VMEM(fw_value.shape, bf),
            pltpu.VMEM(fast_weights.shape, bf),
            pltpu.VMEM(attn_query.shape, bf),
            pltpu.VMEM((span, kv_width), bf),
            pltpu.VMEM((span, kv_width), bf),
            pltpu.VMEM((heads, 3, width, width), bf),
            pltpu.VMEM((heads, 3, width, 2 * LANES), bf),
            pltpu.VMEM((pieces, width, LANES), bf),
            pltpu.VMEM((pieces, width, LANES), bf),
            pltpu.VMEM((pieces, width, LANES), bf),
            pltpu.VMEM((pieces, 2, width, LANES), bf),
            pltpu.VMEM((heads, 3, width, width), bf),
            pltpu.VMEM(attn_query.shape, f32),
            pltpu.VMEM((rows, span), f32),
            pltpu.VMEM((heads, tokens, width), bf),
            pltpu.VMEM((heads, rows, width), bf),
            pltpu.VMEM((heads, rows, width), bf),
            pltpu.VMEM((heads, tokens), f32),
            pltpu.VMEM((heads, tokens, LANES), f32),
            pltpu.VMEM((2, rows, (KV_HEADS - DIRECT) * LANES), bf),
            dma((heads, 3)), dma((5,)), dma((4, KV_HEADS)), dma((4, KV_HEADS)),
            dma((heads, 3)), dma((heads, 3)), *[dma((pieces, SPLIT))] * 6, *[dma((pieces, 2, SPLIT))] * 2,
            *[dma((pieces, SPLIT))] * 6, *[dma((pieces, 2, SPLIT))] * 2,
            *[dma((heads, 3, 2, SPLIT))] * 2, *[dma((heads, 4))] * 2,
            dma((2,)), dma((2,)), dma((2, KV_HEADS - DIRECT)),
        ],
        compiler_params=pltpu.CompilerParams(
            collective_id=0, has_side_effects=True, vmem_limit_bytes=60 * 1024 * 1024
        ),
    )(fw_query, fw_key, fw_value, learn_rate.T, fast_weights, attn_query, attn_key, attn_value)


def takes_fused(mesh, args):
    tokens, rows = args[1].shape[0], args[5].shape[0]
    heads, width = args[4].shape[1], args[4].shape[2]
    return (
        mesh.shape["seq"] == 16
        and mesh.shape["head"] == 2
        and heads == 4
        and width == 4 * LANES
        and tokens == 2 * rows
        and rows < WINDOW < 2 * rows
        and (-(WINDOW + rows)) % LANES > 0
    )


def solution(mesh):
    placed = (
        P("seq", "head"),
        P("seq", "head"),
        P("seq", "head"),
        P("seq", "head"),
        P(None, "head", None, None),
        P(("seq", "head"), None),
        P(("seq", "head"), None),
        P(("seq", "head"), None),
    )

    def body(*args):
        return fused(*args) if takes_fused(mesh, args) else on_device(*args)

    return jax.shard_map(
        body, mesh=mesh, in_specs=placed, out_specs=P(("seq", "head"), None), check_vma=False
    )
```

```python
import functools
import math

import jax
import jax.numpy as jnp
from jax import lax
from jax.experimental import pallas as pl
from jax.experimental.pallas import tpu as pltpu
from jax.sharding import PartitionSpec as P

Q_HEADS = 32
KV_HEADS = 8
HEAD_DIM = 128
WINDOW = 256


def shifted(value, axis, by):
    devices = lax.axis_size(axis)
    pairs = [(i, i + by) for i in range(devices) if 0 <= i + by < devices]
    return lax.ppermute(value, axis, pairs)


def local_grads(keys, values, rates, weights):
    pre_gate = jnp.einsum("thd,hde->the", keys, weights[0], preferred_element_type=jnp.float32)
    pre_up = jnp.einsum("thd,hde->the", keys, weights[1], preferred_element_type=jnp.float32)
    sigm = jax.nn.sigmoid(pre_gate)
    hidden = (pre_gate * sigm * pre_up).astype(jnp.bfloat16)
    scaled = (rates[:, :, None] * values.astype(jnp.float32)).astype(jnp.bfloat16)
    back = jnp.einsum("the,hde->thd", scaled, weights[2], preferred_element_type=jnp.float32)
    d_gate = (back * pre_up * sigm * (1.0 + pre_gate * (1.0 - sigm))).astype(jnp.bfloat16)
    d_up = (back * pre_gate * sigm).astype(jnp.bfloat16)
    grad_gate = jnp.einsum("thd,the->hde", keys, d_gate, preferred_element_type=jnp.float32)
    grad_up = jnp.einsum("thd,the->hde", keys, d_up, preferred_element_type=jnp.float32)
    grad_down = jnp.einsum("thd,the->hde", hidden, scaled, preferred_element_type=jnp.float32)
    return jnp.stack([grad_gate, grad_up, grad_down])


def renorm(summed, start_weights):
    start = start_weights.astype(jnp.float32)
    stepped = start + summed
    ratio = jnp.sqrt(jnp.mean(start * start, axis=-2, keepdims=True)) * lax.rsqrt(
        jnp.mean(stepped * stepped, axis=-2, keepdims=True) + 1e-06
    )
    return (stepped * ratio).astype(jnp.bfloat16)


def on_device(
    fw_query, fw_key, fw_value, learn_rate, fast_weights, attn_query, attn_key, attn_value
):
    tok_rows = fw_key.shape[0]
    local_heads = fast_weights.shape[1]
    width = fast_weights.shape[2]
    keys = fw_key.reshape(tok_rows, local_heads, width)
    values = fw_value.reshape(tok_rows, local_heads, width)
    queries = fw_query.reshape(tok_rows, local_heads, width)
    grads = local_grads(keys, values, learn_rate, fast_weights)
    share = lax.psum_scatter(grads, "seq", scatter_dimension=3, tiled=True)
    columns = share.shape[3]
    start_cols = lax.dynamic_slice_in_dim(fast_weights, lax.axis_index("seq") * columns, columns, 3)
    fresh_part = renorm(share, start_cols)
    fresh = lax.all_gather(fresh_part, "seq", axis=3, tiled=True)
    q_gate = jnp.einsum("thd,hde->the", queries, fresh[0], preferred_element_type=jnp.float32)
    q_up = jnp.einsum("thd,hde->the", queries, fresh[1], preferred_element_type=jnp.float32)
    answer_hidden = (q_gate * jax.nn.sigmoid(q_gate) * q_up).astype(jnp.bfloat16)
    fw_out = jnp.einsum(
        "the,hef->thf", answer_hidden, fresh[2], preferred_element_type=jnp.float32
    ).astype(jnp.bfloat16)
    fw_out = fw_out.reshape(tok_rows, local_heads * width)
    fw_fine = lax.all_to_all(fw_out, "head", split_axis=0, concat_axis=1, tiled=True)
    rows = attn_query.shape[0]
    reach = -(-WINDOW // rows)
    kv_width = attn_key.shape[1]
    group = Q_HEADS // KV_HEADS
    buffer_k = jnp.zeros(((reach + 1) * rows, kv_width), jnp.bfloat16)
    buffer_v = jnp.zeros(((reach + 1) * rows, kv_width), jnp.bfloat16)
    buffer_k = lax.dynamic_update_slice_in_dim(buffer_k, attn_key, reach * rows, 0)
    buffer_v = lax.dynamic_update_slice_in_dim(buffer_v, attn_value, reach * rows, 0)

    def bring(step, carry):
        piece_k, piece_v, store_k, store_v = carry
        piece_k, piece_v = shifted((piece_k, piece_v), ("seq", "head"), 1)
        slot = (reach - 1 - step) * rows
        store_k = lax.dynamic_update_slice_in_dim(store_k, piece_k, slot, 0)
        store_v = lax.dynamic_update_slice_in_dim(store_v, piece_v, slot, 0)
        return (piece_k, piece_v, store_k, store_v)

    carried = lax.fori_loop(0, reach, bring, (attn_key, attn_value, buffer_k, buffer_v))
    buffer_k = carried[2].reshape((reach + 1) * rows, KV_HEADS, HEAD_DIM)
    buffer_v = carried[3].reshape((reach + 1) * rows, KV_HEADS, HEAD_DIM)
    device_pos = lax.axis_index("seq") * lax.axis_size("head") + lax.axis_index("head")
    t_pos = device_pos * rows + jnp.arange(rows, dtype=jnp.int32)
    s_pos = (device_pos - reach) * rows + jnp.arange((reach + 1) * rows, dtype=jnp.int32)
    gap = t_pos[:, None] - s_pos[None, :]
    keep = (gap >= 0) & (gap < WINDOW) & (s_pos[None, :] >= 0)
    query_heads = attn_query.reshape(rows, KV_HEADS, group, HEAD_DIM)
    scaling = 1.0 / math.sqrt(HEAD_DIM)
    scores = (
        jnp.einsum("fcgd,lcd->cgfl", query_heads, buffer_k, preferred_element_type=jnp.float32)
        * scaling
    )
    scores = jnp.where(keep, scores, -1e30)
    top = jnp.max(scores, axis=-1, keepdims=True)
    expo = jnp.exp(scores - top)
    probs = (expo / jnp.sum(expo, axis=-1, keepdims=True)).astype(jnp.bfloat16)
    attn_out = jnp.einsum("cgfl,lcd->fcgd", probs, buffer_v, preferred_element_type=jnp.float32)
    attn_out = attn_out.reshape(rows, Q_HEADS * HEAD_DIM)
    return (attn_out + fw_fine.astype(jnp.float32)).astype(jnp.bfloat16)

MESH = pl.DeviceIdType.MESH
LANES = 128
A_FIRST = 0
DOWN_A_FIRST = 0
LAST_EARLY = 0
SPLIT = 1
LAG_A = 3
ROOT_B = 6
ROOT_A = 6
FIRST_ATT = 4
PREPARE = 2
RELAY_AT = 2
NEAR_AT = -1
FAR_AT = -1
ATT_SPLIT = 0
B_AHEAD = 0


def piece(p):
    return p // 3, p % 3


def fused_kernel(
    heads, width, rows,
    q_hbm, k_hbm, v_hbm, rate_hbm, w_hbm, aq_hbm, ak_hbm, av_hbm, out_ref,
    qb, kb, vb, wb, aqb, akb, avb, g, r0, rxa, rza, rxb, rzb, nw, att, bias, hidb, fsend, frecv, rate_ref, rates, via,
    in_sem, misc_sem, halo_s, halo_r, s0_s, s0_r, xa_s, xa_r, za_s, za_r, xb_s, xb_r, zb_s, zb_r,
    gax_s, gax_r, gaz_s, gaz_r, gbx_s, gbx_r, gbz_s, gbz_r, c_s, c_r, y_s, y_r, via_s, via_r, on_s,
):
    me = lax.axis_index("seq")
    y = lax.axis_index("head")
    n_seq, n_head = lax.axis_size("seq"), lax.axis_size("head")
    core, xx, z = me % 2, (me // 2) % 2, me // 4
    top = n_seq // 4 - 1
    place = z + core * (top - 2 * z)
    cb = core * 2 + xx
    ob = core * 2 + 1 - xx
    other_core = me + 1 - 2 * core
    other_x = me + 2 - 4 * xx
    ahead = me + 4 - 8 * core
    behind = me - 4 + 8 * core
    pos = me * n_head + y
    last = n_seq * n_head
    extra = WINDOW - rows
    pad = akb.shape[0] - WINDOW - rows
    half = 2 * LANES
    pairs = heads // 2
    pieces = pairs * 3
    is_root = place == top

    def cols(block, size=LANES):
        return pl.ds(pl.multiple_of(block * size, size), size)

    def remote(src, dst, ssem, rsem, seq, head=None):
        return pltpu.make_async_remote_copy(
            src_ref=src, dst_ref=dst, send_sem=ssem, recv_sem=rsem,
            device_id={"seq": seq, "head": y if head is None else head},
            device_id_type=MESH,
        )

    def loads(h):
        c = cols(h, width)
        return (
            pltpu.make_async_copy(k_hbm.at[:, c], kb.at[:, c], in_sem.at[h, 0]),
            pltpu.make_async_copy(v_hbm.at[:, c], vb.at[:, c], in_sem.at[h, 1]),
            pltpu.make_async_copy(w_hbm.at[:, h], wb.at[:, h], in_sem.at[h, 2]),
        )

    own_at = pl.ds(pad + WINDOW, rows)
    others = (
        pltpu.make_async_copy(aq_hbm, aqb, misc_sem.at[0]),
        pltpu.make_async_copy(ak_hbm, akb.at[own_at], misc_sem.at[1]),
        pltpu.make_async_copy(av_hbm, avb.at[own_at], misc_sem.at[2]),
        pltpu.make_async_copy(q_hbm, qb, misc_sem.at[3]),
    )
    rate_load = pltpu.make_async_copy(rate_hbm, rate_ref, misc_sem.at[4])
    rate_load.start()
    for i in range(heads):
        for copy in loads(i + 1 - 2 * (i % 2)):
            copy.start()
    for copy in others:
        copy.start()

    barrier = pltpu.get_barrier_semaphore()

    def greet(seq, head):
        pl.semaphore_signal(barrier, inc=1, device_id={"seq": seq, "head": head}, device_id_type=MESH)

    for seq in (other_core, other_x):
        greet(seq, y)
    greet(me, 1 - y)
    below = jnp.where(z > 0, 1, 0)
    above = jnp.where(z < top, 1, 0)

    @pl.when(z > 0)
    def _():
        greet(me - 4, y)

    @pl.when(z < top)
    def _():
        greet(me + 4, y)

    met = 3 + below + above
    for step in (1, 2):
        met = met + jnp.where(pos >= step, 1, 0) + jnp.where(pos + step < last, 1, 0)

        @pl.when(pos + step < last)
        def _():
            greet((pos + step) // n_head, (pos + step) % n_head)

        @pl.when(pos >= step)
        def _():
            greet((pos - step) // n_head, (pos - step) % n_head)

    def place_of(step):
        return (pos + step) // n_head, (pos + step) % n_head

    wide = KV_HEADS // 2 * LANES
    near_at, far_at = pl.ds(pad + extra, rows), pl.ds(pad, extra)

    def near_rows(b):
        return [
            remote(hbm.at[:, cols(b, wide)], ref.at[near_at, cols(b, wide)], halo_s.at[k, b], halo_r.at[k, b], *place_of(1))
            for k, (hbm, ref) in enumerate(((ak_hbm, akb), (av_hbm, avb)))
        ]

    def far_rows():
        return [
            remote(hbm.at[pl.ds(rows - extra, extra)], ref.at[far_at], halo_s.at[k, 2], halo_r.at[k, 2], *place_of(2))
            for k, (hbm, ref) in enumerate(((ak_hbm, akb), (av_hbm, avb)))
        ]

    def spare(k):
        hbm = (ak_hbm, av_hbm)[k]
        return remote(hbm.at[:, cols(1, wide)], via.at[k], via_s.at[k], via_r.at[k], me, 1 - y)

    def onward(k):
        ref = (akb, avb)[k]
        return remote(via.at[k], ref.at[near_at, cols(1, wide)], on_s.at[k], halo_r.at[k, 1], *place_of(2))

    across = core * y
    is_source = (across == 1) & (pos + 1 < last)
    is_relay = (core == 1) & (y == 0) & (pos + 2 < last)

    def near_first():
        @pl.when(pos + 1 < last)
        def _():
            for copy in near_rows(0):
                copy.start()

        @pl.when(is_source)
        def _():
            for k in range(2):
                spare(k).start()

    def near_second():
        @pl.when((pos + 1 < last) & (across == 0))
        def _():
            for copy in near_rows(1):
                copy.start()

    def far_start():
        @pl.when(pos + 2 < last)
        def _():
            for copy in far_rows():
                copy.start()

    def relay_on():
        @pl.when(is_relay)
        def _():
            for k in range(2):
                spare(k).wait_recv()
                onward(k).start()

    depth = width // SPLIT
    bands = range(SPLIT)

    def band(q):
        return pl.ds(q * depth, depth)

    def f32(value):
        return value.astype(jnp.float32)

    def s0(h, m):
        return remote(g.at[h, m, :, cols(1 - core, half)], r0.at[h, m], s0_s.at[h, m], s0_r.at[h, m], other_core)

    def xa(p, q):
        hs, m = piece(p)
        return remote(
            g.at[2 * hs, m, band(q), cols(ob)], rxa.at[p, band(q)], xa_s.at[p, q], xa_r.at[p, q], other_x
        )

    def za(p, q):
        hs, m = piece(p)
        return remote(
            g.at[2 * hs, m, band(q), cols(cb)], rza.at[p, band(q)], za_s.at[p, q], za_r.at[p, q], ahead
        )

    def xb(p, q):
        hs, m = piece(p)
        return remote(
            g.at[2 * hs + 1, m, band(q), cols(ob)], rxb.at[p, band(q)], xb_s.at[p, q], xb_r.at[p, q], other_x
        )

    def zb(p, j, q):
        hs, m = piece(p)
        return remote(
            g.at[2 * hs + 1, m, band(q), cols(core * 2 + j)], rzb.at[p, j, band(q)],
            zb_s.at[p, j, q], zb_r.at[p, j, q], ahead,
        )

    def fresh(h, m, block, q):
        return nw.at[h, m, band(q), cols(block)]

    def gax(p, block, q):
        hs, m = piece(p)
        ref = fresh(2 * hs, m, block, q)
        return remote(ref, ref, gax_s.at[p, q], gax_r.at[p, q], other_x)

    def gaz(p, q):
        hs, m = piece(p)
        ref = fresh(2 * hs, m, cb, q)
        return remote(ref, ref, gaz_s.at[p, q], gaz_r.at[p, q], behind)

    def gbx(p, block, q):
        hs, m = piece(p)
        ref = fresh(2 * hs + 1, m, block, q)
        return remote(ref, ref, gbx_s.at[p, q], gbx_r.at[p, q], other_x)

    def gbz(p, j, q):
        hs, m = piece(p)
        ref = fresh(2 * hs + 1, m, core * 2 + j, q)
        return remote(ref, ref, gbz_s.at[p, j, q], gbz_r.at[p, j, q], behind)

    def pair(h, m, j, q):
        ref = fresh(h, m, core * 2 + j, q)
        return remote(ref, ref, c_s.at[h, m, j, q], c_r.at[h, m, j, q], other_core)

    def pair_from(h, m, j, q):
        ref = fresh(h, m, (1 - core) * 2 + j, q)
        return remote(ref, ref, c_s.at[h, m, j, q], c_r.at[h, m, j, q], other_core)

    def compute(h, send=True):
        for copy in loads(h):
            copy.wait()
        c = cols(h, width)
        keys = kb[:, c]
        rate = rates[h][:, :1]
        scaled = (rate * f32(vb[:, c])).astype(jnp.bfloat16)
        pre_gate = jnp.dot(keys, wb[0, h], preferred_element_type=jnp.float32)
        pre_up = jnp.dot(keys, wb[1, h], preferred_element_type=jnp.float32)
        back = lax.dot_general(
            scaled, wb[2, h], (((1,), (1,)), ((), ())), preferred_element_type=jnp.float32
        )
        sigm = jax.nn.sigmoid(pre_gate)
        tn = (((0,), (0,)), ((), ()))

        def put(m, left, right):
            g[h, m] = lax.dot_general(left, right, tn, preferred_element_type=jnp.float32).astype(g.dtype)
            if send:
                s0(h, m).start()

        d_gate = (back * pre_up * sigm * (1.0 + pre_gate * (1.0 - sigm))).astype(jnp.bfloat16)
        put(0, keys, d_gate)
        d_up = (back * pre_gate * sigm).astype(jnp.bfloat16)
        put(1, keys, d_up)
        hidden = (pre_gate * sigm * pre_up).astype(jnp.bfloat16)
        put(2, hidden, scaled)

    def own(h, m, block, part, q):
        return f32(g[h, m, band(q), cols(block)]) + f32(r0[h, m, band(q), cols(part)])

    def keep_sum(h, m, block, q, value):
        g[h, m, band(q), cols(block)] = value.astype(g.dtype)

    def finish(h, m, total):
        start = f32(wb[m, h, :, cols(cb)])
        stepped = start + total
        ratio = jnp.sqrt(jnp.mean(start * start, axis=0, keepdims=True)) * lax.rsqrt(
            jnp.mean(stepped * stepped, axis=0, keepdims=True) + 1e-06
        )
        nw[h, m, :, cols(cb)] = (stepped * ratio).astype(nw.dtype)

    def own_whole(h, m):
        return f32(g[h, m, :, cols(cb)]) + f32(r0[h, m, :, cols(xx)])

    def stage_in_b(p):
        hs, m = piece(p)
        h = 2 * hs + 1
        s0(h, m).wait_recv()

        @pl.when(place == 0)
        def _():
            for j in range(2):
                for q in bands:
                    keep_sum(h, m, core * 2 + j, q, own(h, m, core * 2 + j, j, q))
                    zb(p, j, q).start()

    def stage_in_a(p):
        hs, m = piece(p)
        h = 2 * hs
        s0(h, m).wait_recv()
        for q in bands:
            keep_sum(h, m, ob, q, own(h, m, ob, 1 - xx, q))
            xa(p, q).start()

    def stage_b(p):
        hs, m = piece(p)
        h = 2 * hs + 1

        @pl.when(place < top)
        def _():
            for j in range(2):
                for q in bands:
                    zb(p, j, q).wait_recv()
                    keep_sum(h, m, core * 2 + j, q, own(h, m, core * 2 + j, j, q) + f32(rzb[p, j, band(q)]))
                    zb(p, j, q).start()

        @pl.when(is_root)
        def _():
            for q in bands:
                zb(p, 1 - xx, q).wait_recv()
                keep_sum(h, m, ob, q, own(h, m, ob, 1 - xx, q) + f32(rzb[p, 1 - xx, band(q)]))
                xb(p, q).start()
            for q in bands:
                zb(p, xx, q).wait_recv()

    def stage_a(p):
        hs, m = piece(p)
        h = 2 * hs

        @pl.when(place == 0)
        def _():
            for q in bands:
                xa(p, q).wait_recv()
                keep_sum(h, m, cb, q, own(h, m, cb, xx, q) + f32(rxa[p, band(q)]))
                za(p, q).start()

        @pl.when((place > 0) & (place < top))
        def _():
            for q in bands:
                xa(p, q).wait_recv()
                za(p, q).wait_recv()
                keep_sum(h, m, cb, q, own(h, m, cb, xx, q) + f32(rxa[p, band(q)]) + f32(rza[p, band(q)]))
                za(p, q).start()

        @pl.when(is_root)
        def _():
            for q in bands:
                xa(p, q).wait_recv()
                za(p, q).wait_recv()

    def stage_root_a(p):
        hs, m = piece(p)
        h = 2 * hs
        finish(h, m, own_whole(h, m) + f32(rxa[p]) + f32(rza[p]))
        for q in bands:
            gaz(p, q).start()
            gax(p, cb, q).start()
            pair(h, m, xx, q).start()

    def stage_root_b(p):
        hs, m = piece(p)
        h = 2 * hs + 1
        for q in bands:
            xb(p, q).wait_recv()
        finish(h, m, own_whole(h, m) + f32(rzb[p, xx]) + f32(rxb[p]))
        for q in bands:
            gbx(p, cb, q).start()
            gbz(p, xx, q).start()
            pair(h, m, xx, q).start()

    def stage_down_a(p):
        hs, m = piece(p)
        for q in bands:
            gaz(p, q).wait_recv()

            @pl.when(place > 0)
            def _():
                gaz(p, q).start()

            gax(p, cb, q).start()
            pair(2 * hs, m, xx, q).start()

    def stage_down_b(p):
        hs, m = piece(p)
        for q in bands:
            gbz(p, xx, q).wait_recv()

            @pl.when(place > 0)
            def _():
                gbz(p, xx, q).start()

            pair(2 * hs + 1, m, xx, q).start()

    def stage_last_b(p):
        hs, m = piece(p)
        for q in bands:
            @pl.when(is_root)
            def _():
                gbx(p, ob, q).wait_recv()
                gbz(p, 1 - xx, q).start()

            @pl.when(place < top)
            def _():
                gbz(p, 1 - xx, q).wait_recv()

                @pl.when(place > 0)
                def _():
                    gbz(p, 1 - xx, q).start()

            pair(2 * hs + 1, m, 1 - xx, q).start()

    def stage_last_a(p):
        hs, m = piece(p)
        for q in bands:
            gax(p, ob, q).wait_recv()
            pair(2 * hs, m, 1 - xx, q).start()

    group = Q_HEADS // KV_HEADS
    scaling = 1.0 / math.sqrt(HEAD_DIM)

    def neighbours_here(c):
        @pl.when((c % (KV_HEADS // 2) == 0) & (pos >= 1))
        def _():
            for copy in near_rows(c // (KV_HEADS // 2)):
                copy.wait_recv()

        @pl.when((c == 0) & (pos >= 2))
        def _():
            for copy in far_rows():
                copy.wait_recv()

    def attend(c, heads_of):
        keys = akb[:, cols(c)]
        vals = avb[:, cols(c)]
        for j in heads_of:
            qc = cols(c * group + j)
            scores = lax.dot_general(
                aqb[:, qc], keys, (((1,), (1,)), ((), ())), preferred_element_type=jnp.float32
            ) * scaling
            scores = jnp.where(bias[...] > 0.0, scores, -1e30)
            peak = jnp.max(scores, axis=-1, keepdims=True)
            expo = jnp.exp(scores - peak)
            probs = (expo / jnp.sum(expo, axis=-1, keepdims=True)).astype(jnp.bfloat16)
            att[:, qc] = jnp.dot(probs, vals, preferred_element_type=jnp.float32)

    def attend_part(t, heads_of):
        c = t - FIRST_ATT

        @pl.when((c >= 0) & (c < KV_HEADS))
        def _():
            if heads_of[0] == 0:
                neighbours_here(c)
            attend(c, heads_of)

    def answer_send(h, block):
        return remote(
            fsend.at[h, :, cols(block)], frecv.at[h, :, cols(block)], y_s.at[h, block], y_r.at[h, block], me, 1 - y
        )

    def mix(value, group_of, h, block):
        at = cols((group_of * heads + h) * 4 + block)
        out_ref[:, at] = (att[:, at] + f32(value)).astype(out_ref.dtype)

    def landed(h, m, j):
        for q in bands:
            pair_from(h, m, j, q).wait_recv()

    def answer_hidden(h):
        for m in range(2):
            for j in range(2):
                landed(h, m, j)
        queries = qb[:, cols(h, width)]
        q_gate = jnp.dot(queries, nw[h, 0], preferred_element_type=jnp.float32)
        q_up = jnp.dot(queries, nw[h, 1], preferred_element_type=jnp.float32)
        hidb[h] = (q_gate * jax.nn.sigmoid(q_gate) * q_up).astype(jnp.bfloat16)

    near_half = place // 2
    early = core * near_half + (1 - core) * (1 - near_half)

    def answer(h, i):
        side = early + (i // 2) * (1 - 2 * early)
        j = xx + (i % 2) * (1 - 2 * xx)
        block = side * 2 + j

        @pl.when(side != core)
        def _():
            landed(h, 2, j)

        part = jnp.dot(hidb[h], nw[h, 2, :, cols(block)], preferred_element_type=jnp.float32).astype(jnp.bfloat16)
        low, high = f32(part[:rows]), f32(part[rows:])
        lower = jnp.zeros((rows, LANES), jnp.int32) + y < 1
        fsend[h, :, cols(block)] = jnp.where(lower, high, low).astype(jnp.bfloat16)
        answer_send(h, block).start()
        mix(jnp.where(lower, low, high), y, h, block)

    def during(p, stage):
        @pl.when((p >= 0) & (p < pieces))
        def _():
            stage(p)

    rate_load.wait()
    for h in range(heads):
        rates[h] = jnp.broadcast_to(rate_ref[h : h + 1, :], (LANES, rate_ref.shape[1])).T
    compute(1, send=False)
    pl.semaphore_wait(barrier, met)
    for m in range(3):
        s0(1, m).start()
    for at, go in ((NEAR_AT, near_first), (FAR_AT, far_start), (NEAR_AT, near_second)):
        if at < 0:
            go()
    if B_AHEAD:
        stage_in_b(0)
    compute(0)

    def prepare():
        for step in (1, 2):
            @pl.when(pos < step)
            def _():
                at = pl.ds(pad + extra, rows) if step == 1 else pl.ds(pad, extra)
                akb[at, :] = jnp.zeros((at.size, akb.shape[1]), akb.dtype)
                avb[at, :] = jnp.zeros((at.size, avb.shape[1]), avb.dtype)

        akb[pl.ds(0, pad), :] = jnp.zeros((pad, akb.shape[1]), akb.dtype)
        avb[pl.ds(0, pad), :] = jnp.zeros((pad, avb.shape[1]), avb.dtype)
        t_idx = lax.broadcasted_iota(jnp.int32, bias.shape, 0)
        s_idx = lax.broadcasted_iota(jnp.int32, bias.shape, 1) - (pad + WINDOW)
        gap = t_idx - s_idx
        keep = (gap >= 0) & (gap < WINDOW) & (s_idx + pos * rows >= 0)
        bias[...] = keep.astype(jnp.float32)
        for copy in others:
            copy.wait()

    done = 2 + max(ROOT_A, ROOT_B) + top + 2
    ticks = pieces + max(ROOT_A, ROOT_B) + (n_seq // 4 - 1) + 1

    def tick(t, _):
        during(t + B_AHEAD, stage_in_b)
        during(t, stage_in_a)

        @pl.when(t < heads - 2)
        def _():
            compute(heads - 1 - t)

        for at, go in ((NEAR_AT, near_first), (FAR_AT, far_start), (NEAR_AT, near_second), (RELAY_AT, relay_on)):
            if at >= 0:
                @pl.when(t == at)
                def _():
                    go()


        @pl.when(place > 0)
        def _():
            during(t - place, stage_b)

        during(t - LAG_A - place, stage_a)

        if ATT_SPLIT:
            attend_part(t, range(ATT_SPLIT))

        @pl.when(is_root)
        def _():
            for at, stage in ((ROOT_A, stage_root_a), (ROOT_B, stage_root_b))[:: 1 if A_FIRST else -1]:
                during(t - at, stage)

        @pl.when(place < top)
        def _():
            for at, stage in ((ROOT_A, stage_down_a), (ROOT_B, stage_down_b))[:: 1 if DOWN_A_FIRST else -1]:
                during(t - at - top + place, stage)

        @pl.when(t == ticks - 1)
        def _():
            for h in range(2, heads):
                answer_hidden(h)

        if LAST_EARLY:
            during(t - ROOT_A - 1 - top + place, stage_last_a)
        during(t - ROOT_B - 1 - top + place, stage_last_b)
        if not LAST_EARLY:
            during(t - ROOT_A - 1 - top + place, stage_last_a)

        @pl.when(t == PREPARE)
        def _():
            prepare()

        attend_part(t, range(ATT_SPLIT, group))

        @pl.when((t >= done) & (t < done + 2))
        def _():
            h = t - done
            answer_hidden(h)

            def one(i, _):
                answer(h, i)
                return 0

            lax.fori_loop(0, 4, one, 0)

        return 0

    lax.fori_loop(0, ticks, tick, 0)

    def tail_answer(i, _):
        answer(2 + i % 2, i // 2)
        return 0

    lax.fori_loop(0, 8, tail_answer, 0)

    @pl.when(pos + 1 < last)
    def _():
        for copy in near_rows(0):
            copy.wait_send()

    @pl.when((pos + 1 < last) & (across == 0))
    def _():
        for copy in near_rows(1):
            copy.wait_send()

    @pl.when(pos + 2 < last)
    def _():
        for copy in far_rows():
            copy.wait_send()

    for k in range(2):
        @pl.when(is_source)
        def _():
            spare(k).wait_send()

        @pl.when(is_relay)
        def _():
            onward(k).wait_send()

    def sent(p, _):
        hs, m = piece(p)
        for k in range(2):
            s0(2 * hs + k, m).wait_send()
        for q in bands:
            xa(p, q).wait_send()
            gax(p, cb, q).wait_send()
            for k in range(2):
                for j in range(2):
                    pair(2 * hs + k, m, j, q).wait_send()

        @pl.when(place < top)
        def _():
            for q in bands:
                za(p, q).wait_send()
                for j in range(2):
                    zb(p, j, q).wait_send()

        @pl.when(place > 0)
        def _():
            for q in bands:
                gaz(p, q).wait_send()
                for j in range(2):
                    gbz(p, j, q).wait_send()

        @pl.when(is_root)
        def _():
            for q in bands:
                xb(p, q).wait_send()
                gbx(p, cb, q).wait_send()

        return 0

    lax.fori_loop(0, pieces, sent, 0)

    def arrive(i, _):
        h, k = i // 4, i % 4
        side = early + (k // 2) * (1 - 2 * early)
        block = side * 2 + xx + (k % 2) * (1 - 2 * xx)
        answer_send(h, block).wait_recv()
        mix(frecv[h, :, cols(block)], 1 - y, h, block)
        return 0

    lax.fori_loop(0, heads * 4, arrive, 0)

    def sent_y(i, _):
        answer_send(i // 4, i % 4).wait_send()
        return 0

    lax.fori_loop(0, heads * 4, sent_y, 0)


def fused(fw_query, fw_key, fw_value, learn_rate, fast_weights, attn_query, attn_key, attn_value):
    tokens, heads, width = fw_key.shape[0], fast_weights.shape[1], fast_weights.shape[2]
    rows, kv_width = attn_key.shape
    span = -(-(WINDOW + rows) // LANES) * LANES
    bf, f32 = jnp.bfloat16, jnp.float32
    anywhere = pl.BlockSpec(memory_space=pl.ANY)
    vmem = pl.BlockSpec(memory_space=pltpu.VMEM)
    dma = pltpu.SemaphoreType.DMA
    pieces = heads // 2 * 3
    return pl.pallas_call(
        functools.partial(fused_kernel, heads, width, rows),
        out_shape=pltpu.VMEM(attn_query.shape, bf),
        in_specs=[anywhere, anywhere, anywhere, anywhere, anywhere, anywhere, anywhere, anywhere],
        out_specs=vmem,
        scratch_shapes=[
            pltpu.VMEM(fw_query.shape, bf),
            pltpu.VMEM(fw_key.shape, bf),
            pltpu.VMEM(fw_value.shape, bf),
            pltpu.VMEM(fast_weights.shape, bf),
            pltpu.VMEM(attn_query.shape, bf),
            pltpu.VMEM((span, kv_width), bf),
            pltpu.VMEM((span, kv_width), bf),
            pltpu.VMEM((heads, 3, width, width), bf),
            pltpu.VMEM((heads, 3, width, 2 * LANES), bf),
            pltpu.VMEM((pieces, width, LANES), bf),
            pltpu.VMEM((pieces, width, LANES), bf),
            pltpu.VMEM((pieces, width, LANES), bf),
            pltpu.VMEM((pieces, 2, width, LANES), bf),
            pltpu.VMEM((heads, 3, width, width), bf),
            pltpu.VMEM(attn_query.shape, f32),
            pltpu.VMEM((rows, span), f32),
            pltpu.VMEM((heads, tokens, width), bf),
            pltpu.VMEM((heads, rows, width), bf),
            pltpu.VMEM((heads, rows, width), bf),
            pltpu.VMEM((heads, tokens), f32),
            pltpu.VMEM((heads, tokens, LANES), f32),
            pltpu.VMEM((2, rows, kv_width // 2), bf),
            dma((heads, 3)), dma((5,)), dma((2, 3)), dma((2, 3)),
            dma((heads, 3)), dma((heads, 3)), *[dma((pieces, SPLIT))] * 6, *[dma((pieces, 2, SPLIT))] * 2,
            *[dma((pieces, SPLIT))] * 6, *[dma((pieces, 2, SPLIT))] * 2,
            *[dma((heads, 3, 2, SPLIT))] * 2, *[dma((heads, 4))] * 2,
            dma((2,)), dma((2,)), dma((2,)),
        ],
        compiler_params=pltpu.CompilerParams(
            collective_id=0, has_side_effects=True, vmem_limit_bytes=60 * 1024 * 1024
        ),
    )(fw_query, fw_key, fw_value, learn_rate.T, fast_weights, attn_query, attn_key, attn_value)


def takes_fused(mesh, args):
    tokens, rows = args[1].shape[0], args[5].shape[0]
    heads, width = args[4].shape[1], args[4].shape[2]
    return (
        mesh.shape["seq"] == 16
        and mesh.shape["head"] == 2
        and heads == 4
        and width == 4 * LANES
        and tokens == 2 * rows
        and rows < WINDOW < 2 * rows
        and (-(WINDOW + rows)) % LANES > 0
    )


def solution(mesh):
    placed = (
        P("seq", "head"),
        P("seq", "head"),
        P("seq", "head"),
        P("seq", "head"),
        P(None, "head", None, None),
        P(("seq", "head"), None),
        P(("seq", "head"), None),
        P(("seq", "head"), None),
    )

    def body(*args):
        return fused(*args) if takes_fused(mesh, args) else on_device(*args)

    return jax.shard_map(
        body, mesh=mesh, in_specs=placed, out_specs=P(("seq", "head"), None), check_vma=False
    )
```

```python
import functools
import math

import jax
import jax.numpy as jnp
from jax import lax
from jax.experimental import pallas as pl
from jax.experimental.pallas import tpu as pltpu
from jax.sharding import PartitionSpec as P

Q_HEADS = 32
KV_HEADS = 8
HEAD_DIM = 128
WINDOW = 256


def shifted(value, axis, by):
    devices = lax.axis_size(axis)
    pairs = [(i, i + by) for i in range(devices) if 0 <= i + by < devices]
    return lax.ppermute(value, axis, pairs)


def local_grads(keys, values, rates, weights):
    pre_gate = jnp.einsum("thd,hde->the", keys, weights[0], preferred_element_type=jnp.float32)
    pre_up = jnp.einsum("thd,hde->the", keys, weights[1], preferred_element_type=jnp.float32)
    sigm = jax.nn.sigmoid(pre_gate)
    hidden = (pre_gate * sigm * pre_up).astype(jnp.bfloat16)
    scaled = (rates[:, :, None] * values.astype(jnp.float32)).astype(jnp.bfloat16)
    back = jnp.einsum("the,hde->thd", scaled, weights[2], preferred_element_type=jnp.float32)
    d_gate = (back * pre_up * sigm * (1.0 + pre_gate * (1.0 - sigm))).astype(jnp.bfloat16)
    d_up = (back * pre_gate * sigm).astype(jnp.bfloat16)
    grad_gate = jnp.einsum("thd,the->hde", keys, d_gate, preferred_element_type=jnp.float32)
    grad_up = jnp.einsum("thd,the->hde", keys, d_up, preferred_element_type=jnp.float32)
    grad_down = jnp.einsum("thd,the->hde", hidden, scaled, preferred_element_type=jnp.float32)
    return jnp.stack([grad_gate, grad_up, grad_down])


def renorm(summed, start_weights):
    start = start_weights.astype(jnp.float32)
    stepped = start + summed
    ratio = jnp.sqrt(jnp.mean(start * start, axis=-2, keepdims=True)) * lax.rsqrt(
        jnp.mean(stepped * stepped, axis=-2, keepdims=True) + 1e-06
    )
    return (stepped * ratio).astype(jnp.bfloat16)


def on_device(
    fw_query, fw_key, fw_value, learn_rate, fast_weights, attn_query, attn_key, attn_value
):
    tok_rows = fw_key.shape[0]
    local_heads = fast_weights.shape[1]
    width = fast_weights.shape[2]
    keys = fw_key.reshape(tok_rows, local_heads, width)
    values = fw_value.reshape(tok_rows, local_heads, width)
    queries = fw_query.reshape(tok_rows, local_heads, width)
    grads = local_grads(keys, values, learn_rate, fast_weights)
    share = lax.psum_scatter(grads, "seq", scatter_dimension=3, tiled=True)
    columns = share.shape[3]
    start_cols = lax.dynamic_slice_in_dim(fast_weights, lax.axis_index("seq") * columns, columns, 3)
    fresh_part = renorm(share, start_cols)
    fresh = lax.all_gather(fresh_part, "seq", axis=3, tiled=True)
    q_gate = jnp.einsum("thd,hde->the", queries, fresh[0], preferred_element_type=jnp.float32)
    q_up = jnp.einsum("thd,hde->the", queries, fresh[1], preferred_element_type=jnp.float32)
    answer_hidden = (q_gate * jax.nn.sigmoid(q_gate) * q_up).astype(jnp.bfloat16)
    fw_out = jnp.einsum(
        "the,hef->thf", answer_hidden, fresh[2], preferred_element_type=jnp.float32
    ).astype(jnp.bfloat16)
    fw_out = fw_out.reshape(tok_rows, local_heads * width)
    fw_fine = lax.all_to_all(fw_out, "head", split_axis=0, concat_axis=1, tiled=True)
    rows = attn_query.shape[0]
    reach = -(-WINDOW // rows)
    kv_width = attn_key.shape[1]
    group = Q_HEADS // KV_HEADS
    buffer_k = jnp.zeros(((reach + 1) * rows, kv_width), jnp.bfloat16)
    buffer_v = jnp.zeros(((reach + 1) * rows, kv_width), jnp.bfloat16)
    buffer_k = lax.dynamic_update_slice_in_dim(buffer_k, attn_key, reach * rows, 0)
    buffer_v = lax.dynamic_update_slice_in_dim(buffer_v, attn_value, reach * rows, 0)

    def bring(step, carry):
        piece_k, piece_v, store_k, store_v = carry
        piece_k, piece_v = shifted((piece_k, piece_v), ("seq", "head"), 1)
        slot = (reach - 1 - step) * rows
        store_k = lax.dynamic_update_slice_in_dim(store_k, piece_k, slot, 0)
        store_v = lax.dynamic_update_slice_in_dim(store_v, piece_v, slot, 0)
        return (piece_k, piece_v, store_k, store_v)

    carried = lax.fori_loop(0, reach, bring, (attn_key, attn_value, buffer_k, buffer_v))
    buffer_k = carried[2].reshape((reach + 1) * rows, KV_HEADS, HEAD_DIM)
    buffer_v = carried[3].reshape((reach + 1) * rows, KV_HEADS, HEAD_DIM)
    device_pos = lax.axis_index("seq") * lax.axis_size("head") + lax.axis_index("head")
    t_pos = device_pos * rows + jnp.arange(rows, dtype=jnp.int32)
    s_pos = (device_pos - reach) * rows + jnp.arange((reach + 1) * rows, dtype=jnp.int32)
    gap = t_pos[:, None] - s_pos[None, :]
    keep = (gap >= 0) & (gap < WINDOW) & (s_pos[None, :] >= 0)
    query_heads = attn_query.reshape(rows, KV_HEADS, group, HEAD_DIM)
    scaling = 1.0 / math.sqrt(HEAD_DIM)
    scores = (
        jnp.einsum("fcgd,lcd->cgfl", query_heads, buffer_k, preferred_element_type=jnp.float32)
        * scaling
    )
    scores = jnp.where(keep, scores, -1e30)
    top = jnp.max(scores, axis=-1, keepdims=True)
    expo = jnp.exp(scores - top)
    probs = (expo / jnp.sum(expo, axis=-1, keepdims=True)).astype(jnp.bfloat16)
    attn_out = jnp.einsum("cgfl,lcd->fcgd", probs, buffer_v, preferred_element_type=jnp.float32)
    attn_out = attn_out.reshape(rows, Q_HEADS * HEAD_DIM)
    return (attn_out + fw_fine.astype(jnp.float32)).astype(jnp.bfloat16)

MESH = pl.DeviceIdType.MESH
LANES = 128
TURN = 1
A_FIRST = 0
DOWN_A_FIRST = 0
LAST_EARLY = 0
SPLIT = 1
LAG_A = 3
ROOT_B = 6
ROOT_A = 6
FIRST_ATT = 4
PREPARE = 2
RELAY_AT = 2
NEAR_AT = -1
FAR_AT = -1
ATT_SPLIT = 0
B_AHEAD = 0


def piece(p):
    return p // 3, p % 3


def fused_kernel(
    heads, width, rows,
    q_hbm, k_hbm, v_hbm, rate_hbm, w_hbm, aq_hbm, ak_hbm, av_hbm, out_ref,
    qb, kb, vb, wb, aqb, akb, avb, g, r0, rxa, rza, rxb, rzb, nw, att, bias, hidb, fsend, frecv, rate_ref, rates, via,
    in_sem, misc_sem, halo_s, halo_r, s0_s, s0_r, xa_s, xa_r, za_s, za_r, xb_s, xb_r, zb_s, zb_r,
    gax_s, gax_r, gaz_s, gaz_r, gbx_s, gbx_r, gbz_s, gbz_r, c_s, c_r, y_s, y_r, via_s, via_r, on_s,
):
    me = lax.axis_index("seq")
    y = lax.axis_index("head")
    n_seq, n_head = lax.axis_size("seq"), lax.axis_size("head")
    core, xx, z = me % 2, (me // 2) % 2, me // 4
    top = n_seq // 4 - 1
    place = z + ((1 - TURN) // 2 + core * TURN) * (top - 2 * z)
    cb = core * 2 + xx
    ob = core * 2 + 1 - xx
    other_core = me + 1 - 2 * core
    other_x = me + 2 - 4 * xx
    ahead = (me + n_seq + (4 - 8 * core) * TURN) % n_seq
    behind = (me + n_seq - (4 - 8 * core) * TURN) % n_seq
    pos = me * n_head + y
    last = n_seq * n_head
    extra = WINDOW - rows
    pad = akb.shape[0] - WINDOW - rows
    half = 2 * LANES
    pairs = heads // 2
    pieces = pairs * 3
    is_root = place == top

    def cols(block, size=LANES):
        return pl.ds(pl.multiple_of(block * size, size), size)

    def remote(src, dst, ssem, rsem, seq, head=None):
        return pltpu.make_async_remote_copy(
            src_ref=src, dst_ref=dst, send_sem=ssem, recv_sem=rsem,
            device_id={"seq": seq, "head": y if head is None else head},
            device_id_type=MESH,
        )

    def loads(h):
        c = cols(h, width)
        return (
            pltpu.make_async_copy(k_hbm.at[:, c], kb.at[:, c], in_sem.at[h, 0]),
            pltpu.make_async_copy(v_hbm.at[:, c], vb.at[:, c], in_sem.at[h, 1]),
            pltpu.make_async_copy(w_hbm.at[:, h], wb.at[:, h], in_sem.at[h, 2]),
        )

    own_at = pl.ds(pad + WINDOW, rows)
    others = (
        pltpu.make_async_copy(aq_hbm, aqb, misc_sem.at[0]),
        pltpu.make_async_copy(ak_hbm, akb.at[own_at], misc_sem.at[1]),
        pltpu.make_async_copy(av_hbm, avb.at[own_at], misc_sem.at[2]),
        pltpu.make_async_copy(q_hbm, qb, misc_sem.at[3]),
    )
    rate_load = pltpu.make_async_copy(rate_hbm, rate_ref, misc_sem.at[4])
    rate_load.start()
    for i in range(heads):
        for copy in loads(i + 1 - 2 * (i % 2)):
            copy.start()
    for copy in others:
        copy.start()

    barrier = pltpu.get_barrier_semaphore()

    def greet(seq, head):
        pl.semaphore_signal(barrier, inc=1, device_id={"seq": seq, "head": head}, device_id_type=MESH)

    for seq in (other_core, other_x):
        greet(seq, y)
    greet(me, 1 - y)
    below = jnp.where(z > 0, 1, 0)
    above = jnp.where(z < top, 1, 0)

    @pl.when(z > 0)
    def _():
        greet(me - 4, y)

    @pl.when(z < top)
    def _():
        greet(me + 4, y)

    met = 3 + below + above
    for step in (1, 2):
        met = met + jnp.where(pos >= step, 1, 0) + jnp.where(pos + step < last, 1, 0)

        @pl.when(pos + step < last)
        def _():
            greet((pos + step) // n_head, (pos + step) % n_head)

        @pl.when(pos >= step)
        def _():
            greet((pos - step) // n_head, (pos - step) % n_head)

    def place_of(step):
        there = (pos + step) % last
        return there // n_head, there % n_head

    wide = KV_HEADS // 2 * LANES
    near_at, far_at = pl.ds(pad + extra, rows), pl.ds(pad, extra)

    def near_rows(b):
        return [
            remote(hbm.at[:, cols(b, wide)], ref.at[near_at, cols(b, wide)], halo_s.at[k, b], halo_r.at[k, b], *place_of(1))
            for k, (hbm, ref) in enumerate(((ak_hbm, akb), (av_hbm, avb)))
        ]

    def far_rows():
        return [
            remote(hbm.at[pl.ds(rows - extra, extra)], ref.at[far_at], halo_s.at[k, 2], halo_r.at[k, 2], *place_of(2))
            for k, (hbm, ref) in enumerate(((ak_hbm, akb), (av_hbm, avb)))
        ]

    def spare(k):
        hbm = (ak_hbm, av_hbm)[k]
        return remote(hbm.at[:, cols(1, wide)], via.at[k], via_s.at[k], via_r.at[k], me, 1 - y)

    def onward(k):
        ref = (akb, avb)[k]
        return remote(via.at[k], ref.at[near_at, cols(1, wide)], on_s.at[k], halo_r.at[k, 1], *place_of(2))

    across = core * y
    is_source = (across == 1) & (pos + 1 < last)
    is_relay = (core == 1) & (y == 0) & (pos + 2 < last)

    def near_first():
        @pl.when(pos + 1 < last)
        def _():
            for copy in near_rows(0):
                copy.start()

        @pl.when(is_source)
        def _():
            for k in range(2):
                spare(k).start()

    def near_second():
        @pl.when((pos + 1 < last) & (across == 0))
        def _():
            for copy in near_rows(1):
                copy.start()

    def far_start():
        @pl.when(pos + 2 < last)
        def _():
            for copy in far_rows():
                copy.start()

    def relay_on():
        @pl.when(is_relay)
        def _():
            for k in range(2):
                spare(k).wait_recv()
                onward(k).start()

    depth = width // SPLIT
    bands = range(SPLIT)

    def band(q):
        return pl.ds(q * depth, depth)

    def f32(value):
        return value.astype(jnp.float32)

    def s0(h, m):
        return remote(g.at[h, m, :, cols(1 - core, half)], r0.at[h, m], s0_s.at[h, m], s0_r.at[h, m], other_core)

    def xa(p, q):
        hs, m = piece(p)
        return remote(
            g.at[2 * hs, m, band(q), cols(ob)], rxa.at[p, band(q)], xa_s.at[p, q], xa_r.at[p, q], other_x
        )

    def za(p, q):
        hs, m = piece(p)
        return remote(
            g.at[2 * hs, m, band(q), cols(cb)], rza.at[p, band(q)], za_s.at[p, q], za_r.at[p, q], ahead
        )

    def xb(p, q):
        hs, m = piece(p)
        return remote(
            g.at[2 * hs + 1, m, band(q), cols(ob)], rxb.at[p, band(q)], xb_s.at[p, q], xb_r.at[p, q], other_x
        )

    def zb(p, j, q):
        hs, m = piece(p)
        return remote(
            g.at[2 * hs + 1, m, band(q), cols(core * 2 + j)], rzb.at[p, j, band(q)],
            zb_s.at[p, j, q], zb_r.at[p, j, q], ahead,
        )

    def fresh(h, m, block, q):
        return nw.at[h, m, band(q), cols(block)]

    def gax(p, block, q):
        hs, m = piece(p)
        ref = fresh(2 * hs, m, block, q)
        return remote(ref, ref, gax_s.at[p, q], gax_r.at[p, q], other_x)

    def gaz(p, q):
        hs, m = piece(p)
        ref = fresh(2 * hs, m, cb, q)
        return remote(ref, ref, gaz_s.at[p, q], gaz_r.at[p, q], behind)

    def gbx(p, block, q):
        hs, m = piece(p)
        ref = fresh(2 * hs + 1, m, block, q)
        return remote(ref, ref, gbx_s.at[p, q], gbx_r.at[p, q], other_x)

    def gbz(p, j, q):
        hs, m = piece(p)
        ref = fresh(2 * hs + 1, m, core * 2 + j, q)
        return remote(ref, ref, gbz_s.at[p, j, q], gbz_r.at[p, j, q], behind)

    def pair(h, m, j, q):
        ref = fresh(h, m, core * 2 + j, q)
        return remote(ref, ref, c_s.at[h, m, j, q], c_r.at[h, m, j, q], other_core)

    def pair_from(h, m, j, q):
        ref = fresh(h, m, (1 - core) * 2 + j, q)
        return remote(ref, ref, c_s.at[h, m, j, q], c_r.at[h, m, j, q], other_core)

    def compute(h, send=True):
        for copy in loads(h):
            copy.wait()
        c = cols(h, width)
        keys = kb[:, c]
        rate = rates[h][:, :1]
        scaled = (rate * f32(vb[:, c])).astype(jnp.bfloat16)
        pre_gate = jnp.dot(keys, wb[0, h], preferred_element_type=jnp.float32)
        pre_up = jnp.dot(keys, wb[1, h], preferred_element_type=jnp.float32)
        back = lax.dot_general(
            scaled, wb[2, h], (((1,), (1,)), ((), ())), preferred_element_type=jnp.float32
        )
        sigm = jax.nn.sigmoid(pre_gate)
        tn = (((0,), (0,)), ((), ()))

        def put(m, left, right):
            g[h, m] = lax.dot_general(left, right, tn, preferred_element_type=jnp.float32).astype(g.dtype)
            if send:
                s0(h, m).start()

        d_gate = (back * pre_up * sigm * (1.0 + pre_gate * (1.0 - sigm))).astype(jnp.bfloat16)
        put(0, keys, d_gate)
        d_up = (back * pre_gate * sigm).astype(jnp.bfloat16)
        put(1, keys, d_up)
        hidden = (pre_gate * sigm * pre_up).astype(jnp.bfloat16)
        put(2, hidden, scaled)

    def own(h, m, block, part, q):
        return f32(g[h, m, band(q), cols(block)]) + f32(r0[h, m, band(q), cols(part)])

    def keep_sum(h, m, block, q, value):
        g[h, m, band(q), cols(block)] = value.astype(g.dtype)

    def finish(h, m, total):
        start = f32(wb[m, h, :, cols(cb)])
        stepped = start + total
        ratio = jnp.sqrt(jnp.mean(start * start, axis=0, keepdims=True)) * lax.rsqrt(
            jnp.mean(stepped * stepped, axis=0, keepdims=True) + 1e-06
        )
        nw[h, m, :, cols(cb)] = (stepped * ratio).astype(nw.dtype)

    def own_whole(h, m):
        return f32(g[h, m, :, cols(cb)]) + f32(r0[h, m, :, cols(xx)])

    def stage_in_b(p):
        hs, m = piece(p)
        h = 2 * hs + 1
        s0(h, m).wait_recv()

        @pl.when(place == 0)
        def _():
            for j in range(2):
                for q in bands:
                    keep_sum(h, m, core * 2 + j, q, own(h, m, core * 2 + j, j, q))
                    zb(p, j, q).start()

    def stage_in_a(p):
        hs, m = piece(p)
        h = 2 * hs
        s0(h, m).wait_recv()
        for q in bands:
            keep_sum(h, m, ob, q, own(h, m, ob, 1 - xx, q))
            xa(p, q).start()

    def stage_b(p):
        hs, m = piece(p)
        h = 2 * hs + 1

        @pl.when(place < top)
        def _():
            for j in range(2):
                for q in bands:
                    zb(p, j, q).wait_recv()
                    keep_sum(h, m, core * 2 + j, q, own(h, m, core * 2 + j, j, q) + f32(rzb[p, j, band(q)]))
                    zb(p, j, q).start()

        @pl.when(is_root)
        def _():
            for q in bands:
                zb(p, 1 - xx, q).wait_recv()
                keep_sum(h, m, ob, q, own(h, m, ob, 1 - xx, q) + f32(rzb[p, 1 - xx, band(q)]))
                xb(p, q).start()
            for q in bands:
                zb(p, xx, q).wait_recv()

    def stage_a(p):
        hs, m = piece(p)
        h = 2 * hs

        @pl.when(place == 0)
        def _():
            for q in bands:
                xa(p, q).wait_recv()
                keep_sum(h, m, cb, q, own(h, m, cb, xx, q) + f32(rxa[p, band(q)]))
                za(p, q).start()

        @pl.when((place > 0) & (place < top))
        def _():
            for q in bands:
                xa(p, q).wait_recv()
                za(p, q).wait_recv()
                keep_sum(h, m, cb, q, own(h, m, cb, xx, q) + f32(rxa[p, band(q)]) + f32(rza[p, band(q)]))
                za(p, q).start()

        @pl.when(is_root)
        def _():
            for q in bands:
                xa(p, q).wait_recv()
                za(p, q).wait_recv()

    def stage_root_a(p):
        hs, m = piece(p)
        h = 2 * hs
        finish(h, m, own_whole(h, m) + f32(rxa[p]) + f32(rza[p]))
        for q in bands:
            gaz(p, q).start()
            gax(p, cb, q).start()
            pair(h, m, xx, q).start()

    def stage_root_b(p):
        hs, m = piece(p)
        h = 2 * hs + 1
        for q in bands:
            xb(p, q).wait_recv()
        finish(h, m, own_whole(h, m) + f32(rzb[p, xx]) + f32(rxb[p]))
        for q in bands:
            gbx(p, cb, q).start()
            gbz(p, xx, q).start()
            pair(h, m, xx, q).start()

    def stage_down_a(p):
        hs, m = piece(p)
        for q in bands:
            gaz(p, q).wait_recv()

            @pl.when(place > 0)
            def _():
                gaz(p, q).start()

            gax(p, cb, q).start()
            pair(2 * hs, m, xx, q).start()

    def stage_down_b(p):
        hs, m = piece(p)
        for q in bands:
            gbz(p, xx, q).wait_recv()

            @pl.when(place > 0)
            def _():
                gbz(p, xx, q).start()

            pair(2 * hs + 1, m, xx, q).start()

    def stage_last_b(p):
        hs, m = piece(p)
        for q in bands:
            @pl.when(is_root)
            def _():
                gbx(p, ob, q).wait_recv()
                gbz(p, 1 - xx, q).start()

            @pl.when(place < top)
            def _():
                gbz(p, 1 - xx, q).wait_recv()

                @pl.when(place > 0)
                def _():
                    gbz(p, 1 - xx, q).start()

            pair(2 * hs + 1, m, 1 - xx, q).start()

    def stage_last_a(p):
        hs, m = piece(p)
        for q in bands:
            gax(p, ob, q).wait_recv()
            pair(2 * hs, m, 1 - xx, q).start()

    group = Q_HEADS // KV_HEADS
    scaling = 1.0 / math.sqrt(HEAD_DIM)

    def neighbours_here(c):
        @pl.when((c % (KV_HEADS // 2) == 0) & (pos >= 1))
        def _():
            for copy in near_rows(c // (KV_HEADS // 2)):
                copy.wait_recv()

        @pl.when((c == 0) & (pos >= 2))
        def _():
            for copy in far_rows():
                copy.wait_recv()

    def attend(c, heads_of):
        keys = akb[:, cols(c)]
        vals = avb[:, cols(c)]
        for j in heads_of:
            qc = cols(c * group + j)
            scores = lax.dot_general(
                aqb[:, qc], keys, (((1,), (1,)), ((), ())), preferred_element_type=jnp.float32
            ) * scaling
            scores = jnp.where(bias[...] > 0.0, scores, -1e30)
            peak = jnp.max(scores, axis=-1, keepdims=True)
            expo = jnp.exp(scores - peak)
            probs = (expo / jnp.sum(expo, axis=-1, keepdims=True)).astype(jnp.bfloat16)
            att[:, qc] = jnp.dot(probs, vals, preferred_element_type=jnp.float32)

    def attend_part(t, heads_of):
        c = t - FIRST_ATT

        @pl.when((c >= 0) & (c < KV_HEADS))
        def _():
            if heads_of[0] == 0:
                neighbours_here(c)
            attend(c, heads_of)

    def answer_send(h, block):
        return remote(
            fsend.at[h, :, cols(block)], frecv.at[h, :, cols(block)], y_s.at[h, block], y_r.at[h, block], me, 1 - y
        )

    def mix(value, group_of, h, block):
        at = cols((group_of * heads + h) * 4 + block)
        out_ref[:, at] = (att[:, at] + f32(value)).astype(out_ref.dtype)

    def landed(h, m, j):
        for q in bands:
            pair_from(h, m, j, q).wait_recv()

    def answer_hidden(h):
        for m in range(2):
            for j in range(2):
                landed(h, m, j)
        queries = qb[:, cols(h, width)]
        q_gate = jnp.dot(queries, nw[h, 0], preferred_element_type=jnp.float32)
        q_up = jnp.dot(queries, nw[h, 1], preferred_element_type=jnp.float32)
        hidb[h] = (q_gate * jax.nn.sigmoid(q_gate) * q_up).astype(jnp.bfloat16)

    near_half = place // 2
    early = core * near_half + (1 - core) * (1 - near_half)

    def answer(h, i):
        side = early + (i // 2) * (1 - 2 * early)
        j = xx + (i % 2) * (1 - 2 * xx)
        block = side * 2 + j

        @pl.when(side != core)
        def _():
            landed(h, 2, j)

        part = jnp.dot(hidb[h], nw[h, 2, :, cols(block)], preferred_element_type=jnp.float32).astype(jnp.bfloat16)
        low, high = f32(part[:rows]), f32(part[rows:])
        lower = jnp.zeros((rows, LANES), jnp.int32) + y < 1
        fsend[h, :, cols(block)] = jnp.where(lower, high, low).astype(jnp.bfloat16)
        answer_send(h, block).start()
        mix(jnp.where(lower, low, high), y, h, block)

    def during(p, stage):
        @pl.when((p >= 0) & (p < pieces))
        def _():
            stage(p)

    rate_load.wait()
    for h in range(heads):
        rates[h] = jnp.broadcast_to(rate_ref[h : h + 1, :], (LANES, rate_ref.shape[1])).T
    compute(1, send=False)
    pl.semaphore_wait(barrier, met)
    for m in range(3):
        s0(1, m).start()
    for at, go in ((NEAR_AT, near_first), (FAR_AT, far_start), (NEAR_AT, near_second)):
        if at < 0:
            go()
    if B_AHEAD:
        stage_in_b(0)
    compute(0)

    def prepare():
        for step in (1, 2):
            @pl.when(pos < step)
            def _():
                at = pl.ds(pad + extra, rows) if step == 1 else pl.ds(pad, extra)
                akb[at, :] = jnp.zeros((at.size, akb.shape[1]), akb.dtype)
                avb[at, :] = jnp.zeros((at.size, avb.shape[1]), avb.dtype)

        akb[pl.ds(0, pad), :] = jnp.zeros((pad, akb.shape[1]), akb.dtype)
        avb[pl.ds(0, pad), :] = jnp.zeros((pad, avb.shape[1]), avb.dtype)
        t_idx = lax.broadcasted_iota(jnp.int32, bias.shape, 0)
        s_idx = lax.broadcasted_iota(jnp.int32, bias.shape, 1) - (pad + WINDOW)
        gap = t_idx - s_idx
        keep = (gap >= 0) & (gap < WINDOW) & (s_idx + pos * rows >= 0)
        bias[...] = keep.astype(jnp.float32)
        for copy in others:
            copy.wait()

    done = 2 + max(ROOT_A, ROOT_B) + top + 2
    ticks = pieces + max(ROOT_A, ROOT_B) + (n_seq // 4 - 1) + 1

    def tick(t, _):
        during(t + B_AHEAD, stage_in_b)
        during(t, stage_in_a)

        @pl.when(t < heads - 2)
        def _():
            compute(heads - 1 - t)

        for at, go in ((NEAR_AT, near_first), (FAR_AT, far_start), (NEAR_AT, near_second), (RELAY_AT, relay_on)):
            if at >= 0:
                @pl.when(t == at)
                def _():
                    go()


        @pl.when(place > 0)
        def _():
            during(t - place, stage_b)

        during(t - LAG_A - place, stage_a)

        if ATT_SPLIT:
            attend_part(t, range(ATT_SPLIT))

        @pl.when(is_root)
        def _():
            for at, stage in ((ROOT_A, stage_root_a), (ROOT_B, stage_root_b))[:: 1 if A_FIRST else -1]:
                during(t - at, stage)

        @pl.when(place < top)
        def _():
            for at, stage in ((ROOT_A, stage_down_a), (ROOT_B, stage_down_b))[:: 1 if DOWN_A_FIRST else -1]:
                during(t - at - top + place, stage)

        @pl.when(t == ticks - 1)
        def _():
            for h in range(2, heads):
                answer_hidden(h)

        if LAST_EARLY:
            during(t - ROOT_A - 1 - top + place, stage_last_a)
        during(t - ROOT_B - 1 - top + place, stage_last_b)
        if not LAST_EARLY:
            during(t - ROOT_A - 1 - top + place, stage_last_a)

        @pl.when(t == PREPARE)
        def _():
            prepare()

        attend_part(t, range(ATT_SPLIT, group))

        @pl.when((t >= done) & (t < done + 2))
        def _():
            h = t - done
            answer_hidden(h)

            def one(i, _):
                answer(h, i)
                return 0

            lax.fori_loop(0, 4, one, 0)

        return 0

    lax.fori_loop(0, ticks, tick, 0)

    def tail_answer(i, _):
        answer(2 + i % 2, i // 2)
        return 0

    lax.fori_loop(0, 8, tail_answer, 0)

    @pl.when(pos + 1 < last)
    def _():
        for copy in near_rows(0):
            copy.wait_send()

    @pl.when((pos + 1 < last) & (across == 0))
    def _():
        for copy in near_rows(1):
            copy.wait_send()

    @pl.when(pos + 2 < last)
    def _():
        for copy in far_rows():
            copy.wait_send()

    for k in range(2):
        @pl.when(is_source)
        def _():
            spare(k).wait_send()

        @pl.when(is_relay)
        def _():
            onward(k).wait_send()

    def sent(p, _):
        hs, m = piece(p)
        for k in range(2):
            s0(2 * hs + k, m).wait_send()
        for q in bands:
            xa(p, q).wait_send()
            gax(p, cb, q).wait_send()
            for k in range(2):
                for j in range(2):
                    pair(2 * hs + k, m, j, q).wait_send()

        @pl.when(place < top)
        def _():
            for q in bands:
                za(p, q).wait_send()
                for j in range(2):
                    zb(p, j, q).wait_send()

        @pl.when(place > 0)
        def _():
            for q in bands:
                gaz(p, q).wait_send()
                for j in range(2):
                    gbz(p, j, q).wait_send()

        @pl.when(is_root)
        def _():
            for q in bands:
                xb(p, q).wait_send()
                gbx(p, cb, q).wait_send()

        return 0

    lax.fori_loop(0, pieces, sent, 0)

    def arrive(i, _):
        h, k = i // 4, i % 4
        side = early + (k // 2) * (1 - 2 * early)
        block = side * 2 + xx + (k % 2) * (1 - 2 * xx)
        answer_send(h, block).wait_recv()
        mix(frecv[h, :, cols(block)], 1 - y, h, block)
        return 0

    lax.fori_loop(0, heads * 4, arrive, 0)

    def sent_y(i, _):
        answer_send(i // 4, i % 4).wait_send()
        return 0

    lax.fori_loop(0, heads * 4, sent_y, 0)


def fused(fw_query, fw_key, fw_value, learn_rate, fast_weights, attn_query, attn_key, attn_value):
    tokens, heads, width = fw_key.shape[0], fast_weights.shape[1], fast_weights.shape[2]
    rows, kv_width = attn_key.shape
    span = -(-(WINDOW + rows) // LANES) * LANES
    bf, f32 = jnp.bfloat16, jnp.float32
    anywhere = pl.BlockSpec(memory_space=pl.ANY)
    vmem = pl.BlockSpec(memory_space=pltpu.VMEM)
    dma = pltpu.SemaphoreType.DMA
    pieces = heads // 2 * 3
    return pl.pallas_call(
        functools.partial(fused_kernel, heads, width, rows),
        out_shape=pltpu.VMEM(attn_query.shape, bf),
        in_specs=[anywhere, anywhere, anywhere, anywhere, anywhere, anywhere, anywhere, anywhere],
        out_specs=vmem,
        scratch_shapes=[
            pltpu.VMEM(fw_query.shape, bf),
            pltpu.VMEM(fw_key.shape, bf),
            pltpu.VMEM(fw_value.shape, bf),
            pltpu.VMEM(fast_weights.shape, bf),
            pltpu.VMEM(attn_query.shape, bf),
            pltpu.VMEM((span, kv_width), bf),
            pltpu.VMEM((span, kv_width), bf),
            pltpu.VMEM((heads, 3, width, width), bf),
            pltpu.VMEM((heads, 3, width, 2 * LANES), bf),
            pltpu.VMEM((pieces, width, LANES), bf),
            pltpu.VMEM((pieces, width, LANES), bf),
            pltpu.VMEM((pieces, width, LANES), bf),
            pltpu.VMEM((pieces, 2, width, LANES), bf),
            pltpu.VMEM((heads, 3, width, width), bf),
            pltpu.VMEM(attn_query.shape, f32),
            pltpu.VMEM((rows, span), f32),
            pltpu.VMEM((heads, tokens, width), bf),
            pltpu.VMEM((heads, rows, width), bf),
            pltpu.VMEM((heads, rows, width), bf),
            pltpu.VMEM((heads, tokens), f32),
            pltpu.VMEM((heads, tokens, LANES), f32),
            pltpu.VMEM((2, rows, kv_width // 2), bf),
            dma((heads, 3)), dma((5,)), dma((2, 3)), dma((2, 3)),
            dma((heads, 3)), dma((heads, 3)), *[dma((pieces, SPLIT))] * 6, *[dma((pieces, 2, SPLIT))] * 2,
            *[dma((pieces, SPLIT))] * 6, *[dma((pieces, 2, SPLIT))] * 2,
            *[dma((heads, 3, 2, SPLIT))] * 2, *[dma((heads, 4))] * 2,
            dma((2,)), dma((2,)), dma((2,)),
        ],
        compiler_params=pltpu.CompilerParams(
            collective_id=0, has_side_effects=True, vmem_limit_bytes=60 * 1024 * 1024
        ),
    )(fw_query, fw_key, fw_value, learn_rate.T, fast_weights, attn_query, attn_key, attn_value)


def takes_fused(mesh, args):
    tokens, rows = args[1].shape[0], args[5].shape[0]
    heads, width = args[4].shape[1], args[4].shape[2]
    return (
        mesh.shape["seq"] == 16
        and mesh.shape["head"] == 2
        and heads == 4
        and width == 4 * LANES
        and tokens == 2 * rows
        and rows < WINDOW < 2 * rows
        and (-(WINDOW + rows)) % LANES > 0
    )


def solution(mesh):
    placed = (
        P("seq", "head"),
        P("seq", "head"),
        P("seq", "head"),
        P("seq", "head"),
        P(None, "head", None, None),
        P(("seq", "head"), None),
        P(("seq", "head"), None),
        P(("seq", "head"), None),
    )

    def body(*args):
        return fused(*args) if takes_fused(mesh, args) else on_device(*args)

    return jax.shard_map(
        body, mesh=mesh, in_specs=placed, out_specs=P(("seq", "head"), None), check_vma=False
    )
```

```python
import functools
import math

import jax
import jax.numpy as jnp
from jax import lax
from jax.experimental import pallas as pl
from jax.experimental.pallas import tpu as pltpu
from jax.sharding import PartitionSpec as P

Q_HEADS = 32
KV_HEADS = 8
HEAD_DIM = 128
WINDOW = 256


def shifted(value, axis, by):
    devices = lax.axis_size(axis)
    pairs = [(i, i + by) for i in range(devices) if 0 <= i + by < devices]
    return lax.ppermute(value, axis, pairs)


def local_grads(keys, values, rates, weights):
    pre_gate = jnp.einsum("thd,hde->the", keys, weights[0], preferred_element_type=jnp.float32)
    pre_up = jnp.einsum("thd,hde->the", keys, weights[1], preferred_element_type=jnp.float32)
    sigm = jax.nn.sigmoid(pre_gate)
    hidden = (pre_gate * sigm * pre_up).astype(jnp.bfloat16)
    scaled = (rates[:, :, None] * values.astype(jnp.float32)).astype(jnp.bfloat16)
    back = jnp.einsum("the,hde->thd", scaled, weights[2], preferred_element_type=jnp.float32)
    d_gate = (back * pre_up * sigm * (1.0 + pre_gate * (1.0 - sigm))).astype(jnp.bfloat16)
    d_up = (back * pre_gate * sigm).astype(jnp.bfloat16)
    grad_gate = jnp.einsum("thd,the->hde", keys, d_gate, preferred_element_type=jnp.float32)
    grad_up = jnp.einsum("thd,the->hde", keys, d_up, preferred_element_type=jnp.float32)
    grad_down = jnp.einsum("thd,the->hde", hidden, scaled, preferred_element_type=jnp.float32)
    return jnp.stack([grad_gate, grad_up, grad_down])


def renorm(summed, start_weights):
    start = start_weights.astype(jnp.float32)
    stepped = start + summed
    ratio = jnp.sqrt(jnp.mean(start * start, axis=-2, keepdims=True)) * lax.rsqrt(
        jnp.mean(stepped * stepped, axis=-2, keepdims=True) + 1e-06
    )
    return (stepped * ratio).astype(jnp.bfloat16)


def on_device(
    fw_query, fw_key, fw_value, learn_rate, fast_weights, attn_query, attn_key, attn_value
):
    tok_rows = fw_key.shape[0]
    local_heads = fast_weights.shape[1]
    width = fast_weights.shape[2]
    keys = fw_key.reshape(tok_rows, local_heads, width)
    values = fw_value.reshape(tok_rows, local_heads, width)
    queries = fw_query.reshape(tok_rows, local_heads, width)
    grads = local_grads(keys, values, learn_rate, fast_weights)
    share = lax.psum_scatter(grads, "seq", scatter_dimension=3, tiled=True)
    columns = share.shape[3]
    start_cols = lax.dynamic_slice_in_dim(fast_weights, lax.axis_index("seq") * columns, columns, 3)
    fresh_part = renorm(share, start_cols)
    fresh = lax.all_gather(fresh_part, "seq", axis=3, tiled=True)
    q_gate = jnp.einsum("thd,hde->the", queries, fresh[0], preferred_element_type=jnp.float32)
    q_up = jnp.einsum("thd,hde->the", queries, fresh[1], preferred_element_type=jnp.float32)
    answer_hidden = (q_gate * jax.nn.sigmoid(q_gate) * q_up).astype(jnp.bfloat16)
    fw_out = jnp.einsum(
        "the,hef->thf", answer_hidden, fresh[2], preferred_element_type=jnp.float32
    ).astype(jnp.bfloat16)
    fw_out = fw_out.reshape(tok_rows, local_heads * width)
    fw_fine = lax.all_to_all(fw_out, "head", split_axis=0, concat_axis=1, tiled=True)
    rows = attn_query.shape[0]
    reach = -(-WINDOW // rows)
    kv_width = attn_key.shape[1]
    group = Q_HEADS // KV_HEADS
    buffer_k = jnp.zeros(((reach + 1) * rows, kv_width), jnp.bfloat16)
    buffer_v = jnp.zeros(((reach + 1) * rows, kv_width), jnp.bfloat16)
    buffer_k = lax.dynamic_update_slice_in_dim(buffer_k, attn_key, reach * rows, 0)
    buffer_v = lax.dynamic_update_slice_in_dim(buffer_v, attn_value, reach * rows, 0)

    def bring(step, carry):
        piece_k, piece_v, store_k, store_v = carry
        piece_k, piece_v = shifted((piece_k, piece_v), ("seq", "head"), 1)
        slot = (reach - 1 - step) * rows
        store_k = lax.dynamic_update_slice_in_dim(store_k, piece_k, slot, 0)
        store_v = lax.dynamic_update_slice_in_dim(store_v, piece_v, slot, 0)
        return (piece_k, piece_v, store_k, store_v)

    carried = lax.fori_loop(0, reach, bring, (attn_key, attn_value, buffer_k, buffer_v))
    buffer_k = carried[2].reshape((reach + 1) * rows, KV_HEADS, HEAD_DIM)
    buffer_v = carried[3].reshape((reach + 1) * rows, KV_HEADS, HEAD_DIM)
    device_pos = lax.axis_index("seq") * lax.axis_size("head") + lax.axis_index("head")
    t_pos = device_pos * rows + jnp.arange(rows, dtype=jnp.int32)
    s_pos = (device_pos - reach) * rows + jnp.arange((reach + 1) * rows, dtype=jnp.int32)
    gap = t_pos[:, None] - s_pos[None, :]
    keep = (gap >= 0) & (gap < WINDOW) & (s_pos[None, :] >= 0)
    query_heads = attn_query.reshape(rows, KV_HEADS, group, HEAD_DIM)
    scaling = 1.0 / math.sqrt(HEAD_DIM)
    scores = (
        jnp.einsum("fcgd,lcd->cgfl", query_heads, buffer_k, preferred_element_type=jnp.float32)
        * scaling
    )
    scores = jnp.where(keep, scores, -1e30)
    top = jnp.max(scores, axis=-1, keepdims=True)
    expo = jnp.exp(scores - top)
    probs = (expo / jnp.sum(expo, axis=-1, keepdims=True)).astype(jnp.bfloat16)
    attn_out = jnp.einsum("cgfl,lcd->fcgd", probs, buffer_v, preferred_element_type=jnp.float32)
    attn_out = attn_out.reshape(rows, Q_HEADS * HEAD_DIM)
    return (attn_out + fw_fine.astype(jnp.float32)).astype(jnp.bfloat16)

MESH = pl.DeviceIdType.MESH
LANES = 128
TURN = 1
A_FIRST = 0
DOWN_A_FIRST = 0
LAST_EARLY = 0
SPLIT = 1
LAG_A = 3
ROOT_B = 6
ROOT_A = 6
FIRST_ATT = 5
PREPARE = 2
RELAY_AT = 2
NEAR_AT = -1
FAR_AT = -1
ATT_SPLIT = 0
B_AHEAD = 0
NEAR = 4
PASS_EARLY = 1


def piece(p):
    return p // 3, p % 3


def fused_kernel(
    heads, width, rows,
    q_hbm, k_hbm, v_hbm, rate_hbm, w_hbm, aq_hbm, ak_hbm, av_hbm, out_ref,
    qb, kb, vb, wb, aqb, akb, avb, g, r0, rxa, rza, rxb, rzb, nw, att, bias, hidb, fsend, frecv, rate_ref, rates, via,
    in_sem, misc_sem, halo_s, halo_r, s0_s, s0_r, xa_s, xa_r, za_s, za_r, xb_s, xb_r, zb_s, zb_r,
    gax_s, gax_r, gaz_s, gaz_r, gbx_s, gbx_r, gbz_s, gbz_r, c_s, c_r, y_s, y_r, via_s, via_r, on_s, pass_s,
):
    me = lax.axis_index("seq")
    y = lax.axis_index("head")
    n_seq, n_head = lax.axis_size("seq"), lax.axis_size("head")
    core, xx, z = me % 2, (me // 2) % 2, me // 4
    top = n_seq // 4 - 1
    place = z + ((1 - TURN) // 2 + core * TURN) * (top - 2 * z)
    cb = core * 2 + xx
    ob = core * 2 + 1 - xx
    other_core = me + 1 - 2 * core
    other_x = me + 2 - 4 * xx
    ahead = (me + n_seq + (4 - 8 * core) * TURN) % n_seq
    behind = (me + n_seq - (4 - 8 * core) * TURN) % n_seq
    pos = me * n_head + y
    last = n_seq * n_head
    extra = WINDOW - rows
    pad = akb.shape[0] - WINDOW - rows
    half = 2 * LANES
    pairs = heads // 2
    pieces = pairs * 3
    is_root = place == top

    def cols(block, size=LANES):
        return pl.ds(pl.multiple_of(block * size, size), size)

    def remote(src, dst, ssem, rsem, seq, head=None):
        return pltpu.make_async_remote_copy(
            src_ref=src, dst_ref=dst, send_sem=ssem, recv_sem=rsem,
            device_id={"seq": seq, "head": y if head is None else head},
            device_id_type=MESH,
        )

    def loads(h):
        c = cols(h, width)
        return (
            pltpu.make_async_copy(k_hbm.at[:, c], kb.at[:, c], in_sem.at[h, 0]),
            pltpu.make_async_copy(v_hbm.at[:, c], vb.at[:, c], in_sem.at[h, 1]),
            pltpu.make_async_copy(w_hbm.at[:, h], wb.at[:, h], in_sem.at[h, 2]),
        )

    own_at = pl.ds(pad + WINDOW, rows)
    others = (
        pltpu.make_async_copy(aq_hbm, aqb, misc_sem.at[0]),
        pltpu.make_async_copy(ak_hbm, akb.at[own_at], misc_sem.at[1]),
        pltpu.make_async_copy(av_hbm, avb.at[own_at], misc_sem.at[2]),
        pltpu.make_async_copy(q_hbm, qb, misc_sem.at[3]),
    )
    rate_load = pltpu.make_async_copy(rate_hbm, rate_ref, misc_sem.at[4])
    rate_load.start()
    for i in range(heads):
        for copy in loads(i + 1 - 2 * (i % 2)):
            copy.start()
    for copy in others:
        copy.start()

    barrier = pltpu.get_barrier_semaphore()

    def greet(seq, head):
        pl.semaphore_signal(barrier, inc=1, device_id={"seq": seq, "head": head}, device_id_type=MESH)

    for seq in (other_core, other_x):
        greet(seq, y)
    greet(me, 1 - y)
    below = jnp.where(z > 0, 1, 0)
    above = jnp.where(z < top, 1, 0)

    @pl.when(z > 0)
    def _():
        greet(me - 4, y)

    @pl.when(z < top)
    def _():
        greet(me + 4, y)

    met = 3 + below + above
    for step in (1, 2):
        met = met + jnp.where(pos >= step, 1, 0) + jnp.where(pos + step < last, 1, 0)

        @pl.when(pos + step < last)
        def _():
            greet((pos + step) // n_head, (pos + step) % n_head)

        @pl.when(pos >= step)
        def _():
            greet((pos - step) // n_head, (pos - step) % n_head)

    def place_of(step):
        there = (pos + step) % last
        return there // n_head, there % n_head

    def part(b):
        return pl.ds(b * NEAR * LANES, (b * KV_HEADS + (1 - 2 * b) * NEAR) * LANES)

    near_at, far_at = pl.ds(pad + extra, rows), pl.ds(pad, extra)

    def near_rows(b):
        return [
            remote(hbm.at[:, part(b)], ref.at[near_at, part(b)], halo_s.at[k, b], halo_r.at[k, b], *place_of(1))
            for k, (hbm, ref) in enumerate(((ak_hbm, akb), (av_hbm, avb)))
        ]

    def far_rows(b):
        return [
            remote(
                hbm.at[pl.ds(rows - extra, extra), part(b)], ref.at[far_at, part(b)],
                halo_s.at[k, 2 + b], halo_r.at[k, 2 + b], *place_of(2),
            )
            for k, (hbm, ref) in enumerate(((ak_hbm, akb), (av_hbm, avb)))
        ]

    def pass_rows(b):
        return [
            remote(
                ref.at[pl.ds(pad + rows, extra), part(b)], ref.at[far_at, part(b)],
                pass_s.at[k, b], halo_r.at[k, 2 + b], me, 1 - y,
            )
            for k, ref in enumerate((akb, avb))
        ]

    passes = (core == 0) & (y == 0) & (me > 0)

    def spare(k):
        hbm = (ak_hbm, av_hbm)[k]
        return remote(hbm.at[:, part(1)], via.at[k], via_s.at[k], via_r.at[k], me, 1 - y)

    def onward(k):
        ref = (akb, avb)[k]
        return remote(via.at[k], ref.at[near_at, part(1)], on_s.at[k], halo_r.at[k, 1], *place_of(2))

    across = core * y
    is_source = (across == 1) & (pos + 1 < last)
    is_relay = (core == 1) & (y == 0) & (pos + 2 < last)

    def near_first():
        @pl.when(pos + 1 < last)
        def _():
            for copy in near_rows(0):
                copy.start()

        @pl.when(is_source)
        def _():
            for k in range(2):
                spare(k).start()

    def near_second():
        @pl.when((pos + 1 < last) & (across == 0))
        def _():
            for copy in near_rows(1):
                copy.start()

    def far_start():
        @pl.when((pos + 2 < last) & (across == 0))
        def _():
            for b in range(2):
                for copy in far_rows(b):
                    copy.start()

    def relay_on():
        @pl.when(is_relay)
        def _():
            for k in range(2):
                spare(k).wait_recv()
                onward(k).start()

    depth = width // SPLIT
    bands = range(SPLIT)

    def band(q):
        return pl.ds(q * depth, depth)

    def f32(value):
        return value.astype(jnp.float32)

    def s0(h, m):
        return remote(g.at[h, m, :, cols(1 - core, half)], r0.at[h, m], s0_s.at[h, m], s0_r.at[h, m], other_core)

    def xa(p, q):
        hs, m = piece(p)
        return remote(
            g.at[2 * hs, m, band(q), cols(ob)], rxa.at[p, band(q)], xa_s.at[p, q], xa_r.at[p, q], other_x
        )

    def za(p, q):
        hs, m = piece(p)
        return remote(
            g.at[2 * hs, m, band(q), cols(cb)], rza.at[p, band(q)], za_s.at[p, q], za_r.at[p, q], ahead
        )

    def xb(p, q):
        hs, m = piece(p)
        return remote(
            g.at[2 * hs + 1, m, band(q), cols(ob)], rxb.at[p, band(q)], xb_s.at[p, q], xb_r.at[p, q], other_x
        )

    def zb(p, j, q):
        hs, m = piece(p)
        return remote(
            g.at[2 * hs + 1, m, band(q), cols(core * 2 + j)], rzb.at[p, j, band(q)],
            zb_s.at[p, j, q], zb_r.at[p, j, q], ahead,
        )

    def fresh(h, m, block, q):
        return nw.at[h, m, band(q), cols(block)]

    def gax(p, block, q):
        hs, m = piece(p)
        ref = fresh(2 * hs, m, block, q)
        return remote(ref, ref, gax_s.at[p, q], gax_r.at[p, q], other_x)

    def gaz(p, q):
        hs, m = piece(p)
        ref = fresh(2 * hs, m, cb, q)
        return remote(ref, ref, gaz_s.at[p, q], gaz_r.at[p, q], behind)

    def gbx(p, block, q):
        hs, m = piece(p)
        ref = fresh(2 * hs + 1, m, block, q)
        return remote(ref, ref, gbx_s.at[p, q], gbx_r.at[p, q], other_x)

    def gbz(p, j, q):
        hs, m = piece(p)
        ref = fresh(2 * hs + 1, m, core * 2 + j, q)
        return remote(ref, ref, gbz_s.at[p, j, q], gbz_r.at[p, j, q], behind)

    def pair(h, m, j, q):
        ref = fresh(h, m, core * 2 + j, q)
        return remote(ref, ref, c_s.at[h, m, j, q], c_r.at[h, m, j, q], other_core)

    def pair_from(h, m, j, q):
        ref = fresh(h, m, (1 - core) * 2 + j, q)
        return remote(ref, ref, c_s.at[h, m, j, q], c_r.at[h, m, j, q], other_core)

    def compute(h, send=True):
        for copy in loads(h):
            copy.wait()
        c = cols(h, width)
        keys = kb[:, c]
        rate = rates[h][:, :1]
        scaled = (rate * f32(vb[:, c])).astype(jnp.bfloat16)
        pre_gate = jnp.dot(keys, wb[0, h], preferred_element_type=jnp.float32)
        pre_up = jnp.dot(keys, wb[1, h], preferred_element_type=jnp.float32)
        back = lax.dot_general(
            scaled, wb[2, h], (((1,), (1,)), ((), ())), preferred_element_type=jnp.float32
        )
        sigm = jax.nn.sigmoid(pre_gate)
        tn = (((0,), (0,)), ((), ()))

        def put(m, left, right):
            g[h, m] = lax.dot_general(left, right, tn, preferred_element_type=jnp.float32).astype(g.dtype)
            if send:
                s0(h, m).start()

        d_gate = (back * pre_up * sigm * (1.0 + pre_gate * (1.0 - sigm))).astype(jnp.bfloat16)
        put(0, keys, d_gate)
        d_up = (back * pre_gate * sigm).astype(jnp.bfloat16)
        put(1, keys, d_up)
        hidden = (pre_gate * sigm * pre_up).astype(jnp.bfloat16)
        put(2, hidden, scaled)

    def own(h, m, block, part, q):
        return f32(g[h, m, band(q), cols(block)]) + f32(r0[h, m, band(q), cols(part)])

    def keep_sum(h, m, block, q, value):
        g[h, m, band(q), cols(block)] = value.astype(g.dtype)

    def finish(h, m, total):
        start = f32(wb[m, h, :, cols(cb)])
        stepped = start + total
        ratio = jnp.sqrt(jnp.mean(start * start, axis=0, keepdims=True)) * lax.rsqrt(
            jnp.mean(stepped * stepped, axis=0, keepdims=True) + 1e-06
        )
        nw[h, m, :, cols(cb)] = (stepped * ratio).astype(nw.dtype)

    def own_whole(h, m):
        return f32(g[h, m, :, cols(cb)]) + f32(r0[h, m, :, cols(xx)])

    def stage_in_b(p):
        hs, m = piece(p)
        h = 2 * hs + 1
        s0(h, m).wait_recv()

        @pl.when(place == 0)
        def _():
            for j in range(2):
                for q in bands:
                    keep_sum(h, m, core * 2 + j, q, own(h, m, core * 2 + j, j, q))
                    zb(p, j, q).start()

    def stage_in_a(p):
        hs, m = piece(p)
        h = 2 * hs
        s0(h, m).wait_recv()
        for q in bands:
            keep_sum(h, m, ob, q, own(h, m, ob, 1 - xx, q))
            xa(p, q).start()

    def stage_b(p):
        hs, m = piece(p)
        h = 2 * hs + 1

        @pl.when(place < top)
        def _():
            for j in range(2):
                for q in bands:
                    zb(p, j, q).wait_recv()
                    keep_sum(h, m, core * 2 + j, q, own(h, m, core * 2 + j, j, q) + f32(rzb[p, j, band(q)]))
                    zb(p, j, q).start()

        @pl.when(is_root)
        def _():
            for q in bands:
                zb(p, 1 - xx, q).wait_recv()
                keep_sum(h, m, ob, q, own(h, m, ob, 1 - xx, q) + f32(rzb[p, 1 - xx, band(q)]))
                xb(p, q).start()
            for q in bands:
                zb(p, xx, q).wait_recv()

    def stage_a(p):
        hs, m = piece(p)
        h = 2 * hs

        @pl.when(place == 0)
        def _():
            for q in bands:
                xa(p, q).wait_recv()
                keep_sum(h, m, cb, q, own(h, m, cb, xx, q) + f32(rxa[p, band(q)]))
                za(p, q).start()

        @pl.when((place > 0) & (place < top))
        def _():
            for q in bands:
                xa(p, q).wait_recv()
                za(p, q).wait_recv()
                keep_sum(h, m, cb, q, own(h, m, cb, xx, q) + f32(rxa[p, band(q)]) + f32(rza[p, band(q)]))
                za(p, q).start()

        @pl.when(is_root)
        def _():
            for q in bands:
                xa(p, q).wait_recv()
                za(p, q).wait_recv()

    def stage_root_a(p):
        hs, m = piece(p)
        h = 2 * hs
        finish(h, m, own_whole(h, m) + f32(rxa[p]) + f32(rza[p]))
        for q in bands:
            gaz(p, q).start()
            gax(p, cb, q).start()
            pair(h, m, xx, q).start()

    def stage_root_b(p):
        hs, m = piece(p)
        h = 2 * hs + 1
        for q in bands:
            xb(p, q).wait_recv()
        finish(h, m, own_whole(h, m) + f32(rzb[p, xx]) + f32(rxb[p]))
        for q in bands:
            gbx(p, cb, q).start()
            gbz(p, xx, q).start()
            pair(h, m, xx, q).start()

    def stage_down_a(p):
        hs, m = piece(p)
        for q in bands:
            gaz(p, q).wait_recv()

            @pl.when(place > 0)
            def _():
                gaz(p, q).start()

            gax(p, cb, q).start()
            pair(2 * hs, m, xx, q).start()

    def stage_down_b(p):
        hs, m = piece(p)
        for q in bands:
            gbz(p, xx, q).wait_recv()

            @pl.when(place > 0)
            def _():
                gbz(p, xx, q).start()

            pair(2 * hs + 1, m, xx, q).start()

    def stage_last_b(p):
        hs, m = piece(p)
        for q in bands:
            @pl.when(is_root)
            def _():
                gbx(p, ob, q).wait_recv()
                gbz(p, 1 - xx, q).start()

            @pl.when(place < top)
            def _():
                gbz(p, 1 - xx, q).wait_recv()

                @pl.when(place > 0)
                def _():
                    gbz(p, 1 - xx, q).start()

            pair(2 * hs + 1, m, 1 - xx, q).start()

    def stage_last_a(p):
        hs, m = piece(p)
        for q in bands:
            gax(p, ob, q).wait_recv()
            pair(2 * hs, m, 1 - xx, q).start()

    group = Q_HEADS // KV_HEADS
    scaling = 1.0 / math.sqrt(HEAD_DIM)

    def near_here(b):
        @pl.when(pos >= 1)
        def _():
            for copy in near_rows(b):
                copy.wait_recv()

        @pl.when(passes)
        def _():
            for copy in pass_rows(b):
                copy.start()

    def far_here(b):
        @pl.when(pos >= 2)
        def _():
            for copy in far_rows(b):
                copy.wait_recv()

    def attend(c, heads_of):
        keys = akb[:, cols(c)]
        vals = avb[:, cols(c)]
        for j in heads_of:
            qc = cols(c * group + j)
            scores = lax.dot_general(
                aqb[:, qc], keys, (((1,), (1,)), ((), ())), preferred_element_type=jnp.float32
            ) * scaling
            scores = jnp.where(bias[...] > 0.0, scores, -1e30)
            peak = jnp.max(scores, axis=-1, keepdims=True)
            expo = jnp.exp(scores - peak)
            probs = (expo * (1.0 / jnp.sum(expo, axis=-1, keepdims=True))).astype(jnp.bfloat16)
            att[:, qc] = jnp.dot(probs, vals, preferred_element_type=jnp.float32)

    def attend_part(t, heads_of):
        c = t - FIRST_ATT

        @pl.when((c >= 0) & (c < KV_HEADS))
        def _():
            for b in range(2):
                @pl.when(c == b * NEAR)
                def _():
                    far_here(b)

            attend(c, heads_of)

    def answer_send(h, block):
        return remote(
            fsend.at[h, :, cols(block)], frecv.at[h, :, cols(block)], y_s.at[h, block], y_r.at[h, block], me, 1 - y
        )

    def mix(value, group_of, h, block):
        at = cols((group_of * heads + h) * 4 + block)
        out_ref[:, at] = (att[:, at] + f32(value)).astype(out_ref.dtype)

    def landed(h, m, j):
        for q in bands:
            pair_from(h, m, j, q).wait_recv()

    def answer_hidden(h):
        for m in range(2):
            for j in range(2):
                landed(h, m, j)
        queries = qb[:, cols(h, width)]
        q_gate = jnp.dot(queries, nw[h, 0], preferred_element_type=jnp.float32)
        q_up = jnp.dot(queries, nw[h, 1], preferred_element_type=jnp.float32)
        hidb[h] = (q_gate * jax.nn.sigmoid(q_gate) * q_up).astype(jnp.bfloat16)

    near_half = place // 2
    early = core * near_half + (1 - core) * (1 - near_half)

    def answer(h, i):
        side = early + (i // 2) * (1 - 2 * early)
        j = xx + (i % 2) * (1 - 2 * xx)
        block = side * 2 + j

        @pl.when(side != core)
        def _():
            landed(h, 2, j)

        part = jnp.dot(hidb[h], nw[h, 2, :, cols(block)], preferred_element_type=jnp.float32).astype(jnp.bfloat16)
        low, high = f32(part[:rows]), f32(part[rows:])
        lower = jnp.zeros((rows, LANES), jnp.int32) + y < 1
        fsend[h, :, cols(block)] = jnp.where(lower, high, low).astype(jnp.bfloat16)
        answer_send(h, block).start()
        mix(jnp.where(lower, low, high), y, h, block)

    def during(p, stage):
        @pl.when((p >= 0) & (p < pieces))
        def _():
            stage(p)

    rate_load.wait()
    for h in range(heads):
        rates[h] = jnp.broadcast_to(rate_ref[h : h + 1, :], (LANES, rate_ref.shape[1])).T
    compute(1, send=False)
    pl.semaphore_wait(barrier, met)
    for m in range(3):
        s0(1, m).start()
    for at, go in ((NEAR_AT, near_first), (FAR_AT, far_start), (NEAR_AT, near_second)):
        if at < 0:
            go()
    if B_AHEAD:
        stage_in_b(0)
    compute(0)

    def prepare():
        for step in (1, 2):
            @pl.when(pos < step)
            def _():
                at = pl.ds(pad + extra, rows) if step == 1 else pl.ds(pad, extra)
                akb[at, :] = jnp.zeros((at.size, akb.shape[1]), akb.dtype)
                avb[at, :] = jnp.zeros((at.size, avb.shape[1]), avb.dtype)

        akb[pl.ds(0, pad), :] = jnp.zeros((pad, akb.shape[1]), akb.dtype)
        avb[pl.ds(0, pad), :] = jnp.zeros((pad, avb.shape[1]), avb.dtype)
        t_idx = lax.broadcasted_iota(jnp.int32, bias.shape, 0)
        s_idx = lax.broadcasted_iota(jnp.int32, bias.shape, 1) - (pad + WINDOW)
        gap = t_idx - s_idx
        keep = (gap >= 0) & (gap < WINDOW) & (s_idx + pos * rows >= 0)
        bias[...] = keep.astype(jnp.float32)
        for copy in others:
            copy.wait()

    done = 2 + max(ROOT_A, ROOT_B) + top + 2
    ticks = pieces + max(ROOT_A, ROOT_B) + (n_seq // 4 - 1) + 1

    def tick(t, _):
        during(t + B_AHEAD, stage_in_b)
        during(t, stage_in_a)

        @pl.when(t < heads - 2)
        def _():
            compute(heads - 1 - t)

        for at, go in ((NEAR_AT, near_first), (FAR_AT, far_start), (NEAR_AT, near_second), (RELAY_AT, relay_on)):
            if at >= 0:
                @pl.when(t == at)
                def _():
                    go()


        @pl.when(place > 0)
        def _():
            during(t - place, stage_b)

        during(t - LAG_A - place, stage_a)

        if ATT_SPLIT:
            attend_part(t, range(ATT_SPLIT))

        @pl.when(is_root)
        def _():
            for at, stage in ((ROOT_A, stage_root_a), (ROOT_B, stage_root_b))[:: 1 if A_FIRST else -1]:
                during(t - at, stage)

        @pl.when(place < top)
        def _():
            for at, stage in ((ROOT_A, stage_down_a), (ROOT_B, stage_down_b))[:: 1 if DOWN_A_FIRST else -1]:
                during(t - at - top + place, stage)

        @pl.when(t == ticks - 1)
        def _():
            for h in range(2, heads):
                answer_hidden(h)

        if LAST_EARLY:
            during(t - ROOT_A - 1 - top + place, stage_last_a)
        during(t - ROOT_B - 1 - top + place, stage_last_b)
        if not LAST_EARLY:
            during(t - ROOT_A - 1 - top + place, stage_last_a)

        @pl.when(t == PREPARE)
        def _():
            prepare()

        attend_part(t, range(ATT_SPLIT, group))

        for b in range(2):
            @pl.when(t == FIRST_ATT - 1 - PASS_EARLY + b * NEAR)
            def _():
                near_here(b)


        @pl.when((t >= done) & (t < done + 2))
        def _():
            h = t - done
            answer_hidden(h)

            def one(i, _):
                answer(h, i)
                return 0

            lax.fori_loop(0, 4, one, 0)

        return 0

    lax.fori_loop(0, ticks, tick, 0)

    def tail_answer(i, _):
        answer(2 + i % 2, i // 2)
        return 0

    lax.fori_loop(0, 8, tail_answer, 0)

    @pl.when(pos + 1 < last)
    def _():
        for copy in near_rows(0):
            copy.wait_send()

    @pl.when((pos + 1 < last) & (across == 0))
    def _():
        for copy in near_rows(1):
            copy.wait_send()

    @pl.when((pos + 2 < last) & (across == 0))
    def _():
        for b in range(2):
            for copy in far_rows(b):
                copy.wait_send()

    @pl.when(passes)
    def _():
        for b in range(2):
            for copy in pass_rows(b):
                copy.wait_send()

    for k in range(2):
        @pl.when(is_source)
        def _():
            spare(k).wait_send()

        @pl.when(is_relay)
        def _():
            onward(k).wait_send()

    def sent(p, _):
        hs, m = piece(p)
        for k in range(2):
            s0(2 * hs + k, m).wait_send()
        for q in bands:
            xa(p, q).wait_send()
            gax(p, cb, q).wait_send()
            for k in range(2):
                for j in range(2):
                    pair(2 * hs + k, m, j, q).wait_send()

        @pl.when(place < top)
        def _():
            for q in bands:
                za(p, q).wait_send()
                for j in range(2):
                    zb(p, j, q).wait_send()

        @pl.when(place > 0)
        def _():
            for q in bands:
                gaz(p, q).wait_send()
                for j in range(2):
                    gbz(p, j, q).wait_send()

        @pl.when(is_root)
        def _():
            for q in bands:
                xb(p, q).wait_send()
                gbx(p, cb, q).wait_send()

        return 0

    lax.fori_loop(0, pieces, sent, 0)

    def arrive(i, _):
        h, k = i // 4, i % 4
        side = early + (k // 2) * (1 - 2 * early)
        block = side * 2 + xx + (k % 2) * (1 - 2 * xx)
        answer_send(h, block).wait_recv()
        mix(frecv[h, :, cols(block)], 1 - y, h, block)
        return 0

    lax.fori_loop(0, heads * 4, arrive, 0)

    def sent_y(i, _):
        answer_send(i // 4, i % 4).wait_send()
        return 0

    lax.fori_loop(0, heads * 4, sent_y, 0)


def fused(fw_query, fw_key, fw_value, learn_rate, fast_weights, attn_query, attn_key, attn_value):
    tokens, heads, width = fw_key.shape[0], fast_weights.shape[1], fast_weights.shape[2]
    rows, kv_width = attn_key.shape
    span = -(-(WINDOW + rows) // LANES) * LANES
    bf, f32 = jnp.bfloat16, jnp.float32
    anywhere = pl.BlockSpec(memory_space=pl.ANY)
    vmem = pl.BlockSpec(memory_space=pltpu.VMEM)
    dma = pltpu.SemaphoreType.DMA
    pieces = heads // 2 * 3
    return pl.pallas_call(
        functools.partial(fused_kernel, heads, width, rows),
        out_shape=pltpu.VMEM(attn_query.shape, bf),
        in_specs=[anywhere, anywhere, anywhere, anywhere, anywhere, anywhere, anywhere, anywhere],
        out_specs=vmem,
        scratch_shapes=[
            pltpu.VMEM(fw_query.shape, bf),
            pltpu.VMEM(fw_key.shape, bf),
            pltpu.VMEM(fw_value.shape, bf),
            pltpu.VMEM(fast_weights.shape, bf),
            pltpu.VMEM(attn_query.shape, bf),
            pltpu.VMEM((span, kv_width), bf),
            pltpu.VMEM((span, kv_width), bf),
            pltpu.VMEM((heads, 3, width, width), bf),
            pltpu.VMEM((heads, 3, width, 2 * LANES), bf),
            pltpu.VMEM((pieces, width, LANES), bf),
            pltpu.VMEM((pieces, width, LANES), bf),
            pltpu.VMEM((pieces, width, LANES), bf),
            pltpu.VMEM((pieces, 2, width, LANES), bf),
            pltpu.VMEM((heads, 3, width, width), bf),
            pltpu.VMEM(attn_query.shape, f32),
            pltpu.VMEM((rows, span), f32),
            pltpu.VMEM((heads, tokens, width), bf),
            pltpu.VMEM((heads, rows, width), bf),
            pltpu.VMEM((heads, rows, width), bf),
            pltpu.VMEM((heads, tokens), f32),
            pltpu.VMEM((heads, tokens, LANES), f32),
            pltpu.VMEM((2, rows, (KV_HEADS - NEAR) * LANES), bf),
            dma((heads, 3)), dma((5,)), dma((2, 4)), dma((2, 4)),
            dma((heads, 3)), dma((heads, 3)), *[dma((pieces, SPLIT))] * 6, *[dma((pieces, 2, SPLIT))] * 2,
            *[dma((pieces, SPLIT))] * 6, *[dma((pieces, 2, SPLIT))] * 2,
            *[dma((heads, 3, 2, SPLIT))] * 2, *[dma((heads, 4))] * 2,
            dma((2,)), dma((2,)), dma((2,)), dma((2, 2)),
        ],
        compiler_params=pltpu.CompilerParams(
            collective_id=0, has_side_effects=True, vmem_limit_bytes=60 * 1024 * 1024
        ),
    )(fw_query, fw_key, fw_value, learn_rate.T, fast_weights, attn_query, attn_key, attn_value)


def takes_fused(mesh, args):
    tokens, rows = args[1].shape[0], args[5].shape[0]
    heads, width = args[4].shape[1], args[4].shape[2]
    return (
        mesh.shape["seq"] == 16
        and mesh.shape["head"] == 2
        and heads == 4
        and width == 4 * LANES
        and tokens == 2 * rows
        and rows < WINDOW < 2 * rows
        and (-(WINDOW + rows)) % LANES > 0
    )


def solution(mesh):
    placed = (
        P("seq", "head"),
        P("seq", "head"),
        P("seq", "head"),
        P("seq", "head"),
        P(None, "head", None, None),
        P(("seq", "head"), None),
        P(("seq", "head"), None),
        P(("seq", "head"), None),
    )

    def body(*args):
        return fused(*args) if takes_fused(mesh, args) else on_device(*args)

    return jax.shard_map(
        body, mesh=mesh, in_specs=placed, out_specs=P(("seq", "head"), None), check_vma=False
    )
```
